32 devices in a mesh: ctx: 4 (over y, core), tp: 4 (over z), dp: 2 (over x).
Axes of the slice: x: 2, y: 2, z: 4, core: 2. Of those that a mesh axis runs over, the one named last changes fastest.
Arguments:
- tokens: bfloat16 [3072, 3584], P(('dp', 'ctx'), 'tp'), may hold values from -6 to 6
- expert_ids: int32 [3072, 8], P(('dp', 'ctx')), may hold values from 0 to 255, all different within a row; in each aligned block of 384 rows (0 to 383, 384 to 767, ...) at most 24 rows name the same one
- gate_codes: int32 [3072, 8], P(('dp', 'ctx')), may hold values from 1 to 32767
- up_weight: bfloat16 [4, 3584, 1024], P('ctx', 'tp', 'dp'), may hold values from -0.09375 to 0.09375
- down_weight: bfloat16 [4, 1024, 3584], P('ctx', 'dp', 'tp'), may hold values from -0.1875 to 0.1875
- cotangent: bfloat16 [3072, 3584], P(('dp', 'ctx'), 'tp'), may hold values from -6 to 6
Outputs:
- mixed: bfloat16 [3072, 3584], P(('dp', 'ctx'), 'tp')
- grad_tokens: bfloat16 [3072, 3584], P(('dp', 'ctx'), 'tp')
- grad_up: bfloat16 [4, 3584, 1024], P('ctx', 'tp', 'dp')
- grad_down: bfloat16 [4, 1024, 3584], P('ctx', 'dp', 'tp')
The draws below stay inside these ranges and needn't reach their ends.
Inputs may be any that keep to these rules, and one draw needn't show every extreme that they name: `expert_ids`: each row names 8 different experts; among the 384 rows of one device no expert is named more than 24 times.
All inputs are finite; a program needn't handle non-finite values.
Results may differ from the reference program's by a relative error of at most 0.0066.
Values may be sent and summed in bfloat16 or wider, within the bound.
A program may use at most 64 MiB of HBM per device.

```python
import math
import jax
import jax.numpy as jnp
import numpy as np
from jax import lax

D = 3584
HW = 1024
ALL_EXPERTS = 256
TOPK = 8
TOK_DEV = 384
EXPERTS = 4
CAP = 24
TOKENS = 3072
N_DP = 2


def place_ends(values, own_key, smallest, top_value):
    place = [jax.random.randint(jax.random.fold_in(own_key, axis), (), 0, length) for axis, length in enumerate(values.shape)]
    main_axis = values.shape.index(max(values.shape))
    beside = place[:main_axis] + [(place[main_axis] + 1) % values.shape[main_axis]] + place[main_axis + 1:]
    return values.at[tuple(place)].set(smallest).at[tuple(beside)].set(top_value)


def shard_levels(stream_key, shape, pieces, least, top_value):
    def one(dim, blocks):
        steps = jax.random.uniform(jax.random.fold_in(jax.random.fold_in(stream_key, 6), dim), (blocks,), jnp.float32, least / len(pieces), top_value / len(pieces))
        return jnp.repeat(jnp.exp(steps), shape[dim] // blocks).reshape((-1,) + (1,) * (len(shape) - dim - 1))

    loudness = one(*pieces[0])
    for cut in pieces[1:]:
        loudness = loudness * one(*cut)
    return loudness


def assign_block(own_key, own, number, rows, count, top, reach, slope):
    sequence = jax.random.permutation(own_key, count)
    packed, ordinary = portions_of(count, rows * top, reach, slope, True), portions_of(count, rows * top, reach, slope, False)
    places = jnp.arange(count)

    def named(tallies, turn):
        used = int((tallies > 0).sum())
        fixed = max(1, used // 4)
        passed = fixed + (places - fixed + turn * (used - fixed)) % max(1, count - fixed)
        return jnp.zeros((count,), jnp.int32).at[sequence[jnp.where(places < fixed, places, passed)]].set(jnp.asarray(tallies, jnp.int32))

    tallies = jnp.where(number % 4 == 0, named(packed, number // 4), named(ordinary, number - number // 4 - 1))
    mixed = jax.random.permutation(jax.random.fold_in(own, 3), count)
    source_of, sink = mixed[0:count // 2 * 2:2], mixed[1:count // 2 * 2:2]
    slack = jnp.minimum(tallies[source_of] - 1, reach - tallies[sink]) // 2
    slack = jnp.where((source_of == sequence[0]) | (sink == sequence[0]) | (tallies[sink] == 0), 0, jnp.maximum(slack, 0))
    passed = jax.random.randint(jax.random.fold_in(own, 4), (count // 2,), 0, 1 << 20) % (slack + 1)
    tallies = tallies.at[source_of].add(-passed).at[sink].add(passed)
    members = jnp.searchsorted(jnp.cumsum(tallies), jnp.arange(rows * top), side="right").astype(jnp.int32)
    grid = members.reshape(top, rows).T
    grid = grid[jax.random.permutation(jax.random.fold_in(own, 1), rows)]
    turn = jax.random.randint(jax.random.fold_in(own, 2), (rows, 1), 0, top)
    return jnp.take_along_axis(grid, (jnp.arange(top)[None, :] + turn) % top, axis=1)


def portions_of(amount, total, reach, lean, full):
    weights = [(1 << 20) // math.isqrt(grade ** lean) + 1 for grade in range(1, amount + 1)]
    largest = reach if full else min(reach, max(-(-total // amount), total * weights[0] // sum(weights)))
    least = 1 if total - largest >= amount - 1 else 0
    given, rest = [largest] + [least] * (amount - 1), total - largest - least * (amount - 1)
    while rest > 0:
        free = [i for i in range(1, amount) if given[i] < largest] or [i for i in range(1, amount) if given[i] < reach]
        pool, budget = sum([weights[i] for i in free]), rest
        for i in free:
            addition = min(reach - given[i], max(1, budget * weights[i] // pool), rest)
            given[i] = given[i] + addition
            rest = rest - addition
    return np.array(given)


def normal_values(rng, shape, scale, bound, split=(), held_as=jnp.bfloat16):
    result = jax.random.normal(rng, shape, jnp.float32) * scale
    if len(split) > 0:
        result = shard_levels(rng, shape, split, -0.22, 0.18) * result
    return jnp.clip(result, min=-bound, max=bound).astype(held_as)


def setup_inputs(seed: int = 0) -> dict:
    keys = jax.random.split(jax.random.key(seed), 7)
    tokens = normal_values(keys[0], (TOKENS, D), 1.0, 6.0, ((0, 8), (1, 4)))
    expert_ids_keys = jax.random.split(jax.random.fold_in(keys[1], 1), TOKENS // TOK_DEV)
    expert_ids_turns = jax.random.permutation(jax.random.fold_in(keys[1], 3), TOKENS // TOK_DEV)
    expert_ids = jax.vmap(lambda own, number: assign_block(jax.random.fold_in(keys[1], 2), own, number, TOK_DEV, ALL_EXPERTS, TOPK, CAP, 2))(expert_ids_keys, expert_ids_turns).reshape((TOKENS, TOPK))
    gate_codes = place_ends(jax.random.randint(keys[2], (TOKENS, TOPK), 1, 32768), jax.random.fold_in(keys[2], 1), 1, 32767).astype(jnp.int32)
    up_weight = normal_values(keys[3], (EXPERTS, D, HW), D ** -0.5, 0.09375, ((0, 4), (1, 4), (2, 2)))
    down_weight = normal_values(keys[4], (EXPERTS, HW, D), HW ** -0.5, 0.1875, ((0, 4), (1, 2), (2, 4)))
    cotangent = normal_values(keys[5], (TOKENS, D), 1.0, 6.0, ((0, 8), (1, 4)))
    return {"tokens": tokens, "expert_ids": expert_ids, "gate_codes": gate_codes, "up_weight": up_weight, "down_weight": down_weight, "cotangent": cotangent}


def place_slots(expert_ids, gate_codes, experts, capacity):
    rows_count, picks = expert_ids.shape
    flat_ids = expert_ids.reshape(-1)
    one_hot = (flat_ids[:, None] == jnp.arange(experts, dtype=jnp.int32)[None, :]).astype(jnp.int32)
    before = jnp.cumsum(one_hot, axis=0) - one_hot
    slot_rank = lax.optimization_barrier(jnp.sum(before * one_hot, axis=1))
    inside = flat_ids < experts
    target = jnp.where(inside, flat_ids * capacity + slot_rank, experts * capacity).astype(jnp.int32)
    source = (jnp.arange(rows_count * picks, dtype=jnp.int32) // picks).astype(jnp.int32)
    slot_token = jnp.full((experts * capacity,), rows_count, jnp.int32).at[target].set(source, mode='drop')
    weights = gate_codes.reshape(-1).astype(jnp.float32) / 32768.0
    gate_slot = jnp.zeros((experts * capacity,), jnp.float32).at[target].set(weights, mode='drop')
    return (slot_token, gate_slot)

def silu_grad(values):
    sigma = jax.nn.sigmoid(values)
    return sigma * (1.0 + values * (1.0 - sigma))

def reference(tokens, expert_ids, gate_codes, up_weight, down_weight, cotangent):
    blocks = TOKENS // TOK_DEV
    ids_blocks = expert_ids.reshape(blocks, TOK_DEV, TOPK)
    code_blocks = gate_codes.reshape(blocks, TOK_DEV, TOPK)
    local_token, gate_slot = jax.vmap(lambda first, second: place_slots(first, second, EXPERTS, CAP))(ids_blocks, code_blocks)
    offsets = jnp.arange(blocks, dtype=jnp.int32)[:, None] * TOK_DEV
    global_token = jnp.where(local_token < TOK_DEV, local_token + offsets, TOKENS).astype(jnp.int32)
    global_token = global_token.reshape(blocks, EXPERTS, CAP).transpose(1, 0, 2).reshape(EXPERTS, blocks * CAP)
    gate_table = gate_slot.reshape(blocks, EXPERTS, CAP).transpose(1, 0, 2).reshape(EXPERTS, blocks * CAP)
    padded_x = jnp.concatenate([tokens, jnp.zeros((1, D), tokens.dtype)], axis=0)
    padded_c = jnp.concatenate([cotangent, jnp.zeros((1, D), cotangent.dtype)], axis=0)

    def expert_work(operands):
        index, gate, w_up, w_down = operands
        rows = padded_x[index]
        hidden = jnp.dot(rows, w_up, preferred_element_type=jnp.float32)
        active = jax.nn.silu(hidden).astype(jnp.bfloat16)
        produced = jnp.dot(active, w_down, preferred_element_type=jnp.float32).astype(jnp.bfloat16)
        grad_out = (gate[:, None] * padded_c[index].astype(jnp.float32)).astype(jnp.bfloat16)
        grad_act = jnp.dot(grad_out, w_down.T, preferred_element_type=jnp.float32)
        grad_hid = (grad_act * silu_grad(hidden)).astype(jnp.bfloat16)
        grad_in = jnp.dot(grad_hid, w_up.T, preferred_element_type=jnp.float32).astype(jnp.bfloat16)
        rows_g = rows.reshape(N_DP, -1, D).astype(jnp.float32)
        hid_g = grad_hid.reshape(N_DP, -1, HW).astype(jnp.float32)
        act_g = active.reshape(N_DP, -1, HW).astype(jnp.float32)
        out_g = grad_out.reshape(N_DP, -1, D).astype(jnp.float32)
        part_up = jnp.einsum('grj,gri->gji', rows_g, hid_g).astype(jnp.bfloat16)
        part_down = jnp.einsum('gri,grj->gij', act_g, out_g).astype(jnp.bfloat16)
        part_up, part_down = lax.optimization_barrier((part_up, part_down))
        grad_up = lax.optimization_barrier(jnp.sum(part_up.astype(jnp.float32), axis=0)).astype(jnp.bfloat16)
        grad_down = lax.optimization_barrier(jnp.sum(part_down.astype(jnp.float32), axis=0)).astype(jnp.bfloat16)
        return (produced, grad_in, grad_up, grad_down)
    produced, grad_in, grad_up, grad_down = lax.map(expert_work, (global_token, gate_table, up_weight, down_weight))
    flat_index = global_token.reshape(-1)
    flat_gate = gate_table.reshape(-1)
    mixed = jnp.zeros((TOKENS + 1, D), jnp.float32).at[flat_index].add(flat_gate[:, None] * produced.reshape(-1, D).astype(jnp.float32))
    grad_tokens = jnp.zeros((TOKENS + 1, D), jnp.float32).at[flat_index].add(grad_in.reshape(-1, D).astype(jnp.float32))
    return (mixed[:TOKENS].astype(jnp.bfloat16), grad_tokens[:TOKENS].astype(jnp.bfloat16), grad_up, grad_down)
```

```python
import functools

import jax
import jax.numpy as jnp
from jax import lax
from jax.experimental import pallas as pl
from jax.experimental.pallas import tpu as pltpu
from jax.sharding import PartitionSpec as P

MESH = pl.DeviceIdType.MESH
F32 = jnp.float32
BF16 = jnp.bfloat16
FIRST = (((0,), (0,)), ((), ()))
LAST = (((1,), (1,)), ((), ()))
PLAIN = (((1,), (0,)), ((), ()))
CORES = 2


def dot(a, b, how=PLAIN):
    return lax.dot_general(a, b, how, preferred_element_type=F32)


def units_of(n_dp, n_ctx):
    near = CORES if n_ctx % CORES == 0 else 1
    pairs = [(k, m) for k in range(n_dp) for m in range(n_ctx // near)]
    pairs.sort(key=lambda s: (s[0] > 0) + (s[1] > 0))
    spans = []
    for hops in range(3):
        held = [u for u, s in enumerate(pairs) if (s[0] > 0) + (s[1] > 0) == hops]
        if held:
            spans.append((held[0], len(held)))
    return near, pairs, spans


def kernel(
    n_dp, n_ctx, n_tp, cap,
    ids_hbm, codes_hbm, tok_hbm, cot_hbm, up_hbm, down_hbm,
    mixed, q_recv, pick_t, gup, gdown,
    ids_ref, codes_ref, tok, cot, up, down, x_send, g_send, x_recv, g_recv, x_all, g_all,
    h_send, a_send, h_recv, a_recv, act, ghid, p_send, q_send, p_recv, gate_t,
    in_sem, xs, xr, gs, gr, hs, hr, as_, ar, cs, cr, ds, dr, ps, pr, qs, qr,
):
    near, units, spans = units_of(n_dp, n_ctx)
    d, c, t = lax.axis_index("dp"), lax.axis_index("ctx"), lax.axis_index("tp")
    n_blocks, n_chips = n_dp * n_ctx, n_ctx // near
    me = d * n_ctx + c
    chip, core = c // near, lax.rem(c, near)
    slots = n_ctx * cap
    wide = near * cap
    width = h_send.shape[2]

    loads = [
        pltpu.make_async_copy(src, dst, in_sem.at[i])
        for i, (src, dst) in enumerate((
            (ids_hbm, ids_ref), (codes_hbm, codes_ref), (tok_hbm, tok),
            (cot_hbm, cot), (up_hbm.at[0], up), (down_hbm.at[0], down),
        ))
    ]
    for load in loads[:3]:
        load.start()

    def peer(u, i, sign):
        k, m = units[u]
        g = lax.rem(d + (k if sign > 0 else n_dp - k), n_dp)
        p = lax.rem(chip + (m if sign > 0 else n_chips - m), n_chips)
        e = p * near + lax.rem(core + (i if sign > 0 else near - i), near)
        return g, e, {"dp": g, "ctx": e}

    others = [(u, i) for u in range(len(units)) for i in range(near) if u or i]

    def tp_dev(m):
        j = lax.rem(t + m, n_tp)
        return j, {"tp": j}

    barrier = pltpu.get_barrier_semaphore()
    for u, i in others:
        pl.semaphore_signal(barrier, inc=1, device_id=peer(u, i, 1)[2], device_id_type=MESH)
    for m in range(1, n_tp):
        pl.semaphore_signal(barrier, inc=1, device_id=tp_dev(m)[1], device_id_type=MESH)
    for load in loads[3:]:
        load.start()

    picks, rows = ids_ref.shape
    lane = lax.broadcasted_iota(jnp.int32, (slots, rows), 0)
    lane_e = jnp.zeros((slots, rows), jnp.int32)
    for e in range(1, n_ctx):
        lane_e = lane_e + (lane >= e * cap).astype(jnp.int32)
    lane_s = lane - lane_e * cap
    earlier = (
        lax.broadcasted_iota(jnp.int32, (rows, rows), 0)
        < lax.broadcasted_iota(jnp.int32, (rows, rows), 1)
    ).astype(F32).astype(BF16)
    named = jnp.zeros((slots, rows), jnp.int32)
    code = jnp.zeros((slots, rows), jnp.int32)
    loads[0].wait()
    loads[1].wait()
    ids, codes = ids_ref[...], codes_ref[...]
    for k in range(picks):
        hit = ids[k : k + 1] == lane_e
        named = jnp.where(hit, 1, named)
        code = jnp.where(hit, codes[k : k + 1], code)
    rank = dot(named.astype(F32).astype(BF16), earlier)
    chosen = jnp.where(rank == lane_s.astype(F32), named, 0)
    code = chosen * code
    pick = chosen.astype(F32).astype(BF16)
    high = lax.shift_right_logical(code, 8)
    gate_hi = (high.astype(F32) * (1.0 / 128.0)).astype(BF16)
    gate_lo = ((code - high * 256).astype(F32) * (1.0 / 32768.0)).astype(BF16)

    def remote(src, dst, send, recv, dev):
        return pltpu.make_async_remote_copy(
            src, dst, send, recv, device_id=dev, device_id_type=MESH
        )

    def put_blocks(ref, first, value, count):
        for b in range(count):
            ref[first + b] = value[b * cap : (b + 1) * cap].astype(BF16)

    def join(parts):
        return jnp.concatenate([p.astype(F32) for p in parts], axis=0).astype(BF16)

    def scatter_rows(send, recv, send_sem, recv_sem):
        for u, i in others:
            pos = u * near + i
            _, e, dev = peer(u, i, 1)
            remote(send.at[e], recv.at[pos], send_sem.at[pos], recv_sem.at[pos], dev).start()

    def collect(span, send, recv, recv_sem, into):
        parts = []
        for u in range(span[0], span[0] + span[1]):
            for i in range(near):
                pos = u * near + i
                if pos:
                    remote(
                        recv.at[pos], recv.at[pos], recv_sem.at[pos], recv_sem.at[pos],
                        peer(u, i, -1)[2],
                    ).wait_recv()
                    parts.append(recv[pos])
                else:
                    parts.append(send[c])
        value = join(parts)
        into[at(span)] = value
        return value

    def at(span):
        return slice(span[0] * wide, (span[0] + span[1]) * wide)

    def ds_of(span):
        return pl.ds(span[0] * wide, span[1] * wide)

    def tp_scatter(span, value, send, recv, send_sem, recv_sem):
        for j in range(n_tp):
            send[j, at(span)] = value[:, j * width : (j + 1) * width].astype(BF16)
        for m in range(1, n_tp):
            j, dev = tp_dev(m)
            remote(
                send.at[j, ds_of(span)], recv.at[m, ds_of(span)],
                send_sem.at[span[0], m], recv_sem.at[span[0], m], dev,
            ).start()

    def tp_total(span, send, recv, recv_sem):
        value = send[t, at(span)].astype(F32)
        for m in range(1, n_tp):
            part = recv.at[m, ds_of(span)]
            sem = recv_sem.at[span[0], m]
            remote(part, part, sem, sem, tp_dev(n_tp - m)[1]).wait_recv()
            value = value + recv[m, at(span)].astype(F32)
        return value

    def tp_gather(span, buf, send_sem, recv_sem):
        part = buf.at[t, ds_of(span)]
        for m in range(1, n_tp):
            remote(
                part, part, send_sem.at[span[0], m], recv_sem.at[span[0], m], tp_dev(m)[1]
            ).start()

    def tp_whole(span, buf, recv_sem):
        for m in range(1, n_tp):
            j, dev = tp_dev(n_tp - m)
            part = buf.at[j, ds_of(span)]
            sem = recv_sem.at[span[0], m]
            remote(part, part, sem, sem, dev).wait_recv()
        return jnp.concatenate([buf[j, at(span)] for j in range(n_tp)], axis=1)

    def give_back(span, value, send, recv, send_sem, recv_sem):
        put_blocks(send, span[0] * near, value, span[1] * near)
        for u in range(span[0], span[0] + span[1]):
            for i in range(near):
                pos = u * near + i
                if pos:
                    remote(
                        send.at[pos], recv.at[me], send_sem.at[pos], recv_sem.at[me],
                        peer(u, i, -1)[2],
                    ).start()
                else:
                    recv[me] = send[0]

    def returned(recv, recv_sem):
        for u, i in others:
            g, e, dev = peer(u, i, 1)
            b = g * n_ctx + e
            remote(recv.at[b], recv.at[b], recv_sem.at[b], recv_sem.at[b], dev).wait_recv()

    loads[2].wait()
    put_blocks(x_send, 0, dot(pick, tok[...]), n_ctx)
    pl.semaphore_wait(barrier, len(others) + n_tp - 1)
    scatter_rows(x_send, x_recv, xs, xr)
    loads[3].wait()
    put_blocks(g_send, 0, dot(gate_hi, cot[...]) + dot(gate_lo, cot[...]), n_ctx)
    scatter_rows(g_send, g_recv, gs, gr)

    def start_hidden(span):
        x = collect(span, x_send, x_recv, xr, x_all)
        tp_scatter(span, dot(x, up[...]), h_send, h_recv, hs, hr)

    def start_grad(span):
        g = collect(span, g_send, g_recv, gr, g_all)
        tp_scatter(span, dot(g, down[...], LAST), a_send, a_recv, as_, ar)

    slopes = {}

    def activate(span):
        hidden = tp_total(span, h_send, h_recv, hr)
        sigma = 1.0 / (1.0 + jnp.exp(-hidden))
        act[t, at(span)] = (hidden * sigma).astype(BF16)
        slopes[span] = sigma * (1.0 + hidden * (1.0 - sigma))

    def grade(span):
        ghid[t, at(span)] = (tp_total(span, a_send, a_recv, ar) * slopes[span]).astype(BF16)

    def give_act(span):
        tp_gather(span, act, cs, cr)

    def give_ghid(span):
        tp_gather(span, ghid, ds, dr)

    def produce(span):
        value = dot(tp_whole(span, act, cr), down[...])
        give_back(span, value, p_send, p_recv, ps, pr)

    def to_inputs(span):
        value = dot(tp_whole(span, ghid, dr), up[...], LAST)
        give_back(span, value, q_send, q_recv, qs, qr)

    home, rest = spans[0], spans[1:]
    loads[4].wait()
    start_hidden(home)
    loads[5].wait()
    start_grad(home)
    n_rep = n_dp
    twice = jnp.concatenate([pick.astype(F32)] * n_rep, axis=0)
    pick_t[...] = twice.T.astype(BF16)
    gates = jnp.concatenate(
        [gate_hi.astype(F32)] * n_rep + [gate_lo.astype(F32)] * n_rep, axis=0
    )
    gate_t[...] = gates.T.astype(BF16)
    for span in rest:
        start_hidden(span)
    for span in rest[:1]:
        start_grad(span)
        activate(span)
        give_act(span)
    for span in rest[1:]:
        start_grad(span)
    activate(home)
    grade(home)
    for span in rest[1:]:
        activate(span)
        give_act(span)
    for span in rest[:1]:
        grade(span)
        give_ghid(span)
        produce(span)
    for span in rest[1:]:
        grade(span)
        give_ghid(span)
    give_act(home)
    give_ghid(home)
    for span in rest[1:]:
        produce(span)
    for span in rest:
        to_inputs(span)
    produce(home)
    to_inputs(home)

    def whole(buf):
        return jnp.concatenate([buf[j] for j in range(n_tp)], axis=1)

    gdown[0] = dot(whole(act), g_all[...], FIRST).astype(BF16)
    gup[0] = dot(x_all[...], whole(ghid), FIRST).astype(BF16)

    returned(p_recv, pr)
    got = join([p_recv[b] for b in range(n_blocks)])
    half = n_blocks * cap
    mixed[...] = (dot(gate_t[:, :half], got) + dot(gate_t[:, half:], got)).astype(BF16)
    returned(q_recv, qr)

    for u, i in others:
        pos = u * near + i
        for buf, sem in ((x_send, xs), (g_send, gs), (p_send, ps), (q_send, qs)):
            part = buf.at[0]
            remote(part, part, sem.at[pos], sem.at[pos], peer(u, i, 1)[2]).wait_send()
    for span in spans:
        for m in range(1, n_tp):
            for buf, sem in ((h_send, hs), (a_send, as_), (act, cs), (ghid, ds)):
                part = buf.at[0, ds_of(span)]
                s = sem.at[span[0], m]
                remote(part, part, s, s, tp_dev(m)[1]).wait_send()


def store(n_blocks, mixed, q_recv, pick_t, gup, gdown, mixed_o, gtok_o, gup_o, gdown_o, gtok, sem):
    copies = [
        pltpu.make_async_copy(src, dst, sem.at[i])
        for i, (src, dst) in enumerate(((gup, gup_o), (gdown, gdown_o), (mixed, mixed_o)))
    ]
    for copy in copies:
        copy.start()
    got = jnp.concatenate([q_recv[b].astype(F32) for b in range(n_blocks)], axis=0).astype(BF16)
    rows = gtok.shape[0]
    parts = 3 if rows % 48 == 0 else 1
    step = rows // parts
    for i in range(parts):
        here = slice(i * step, (i + 1) * step)
        gtok[here] = dot(pick_t[here], got).astype(BF16)
        part = pl.ds(i * step, step)
        copy = pltpu.make_async_copy(gtok.at[part], gtok_o.at[part], sem.at[3 + i])
        copy.start()
        copies.append(copy)
    for copy in copies:
        copy.wait()


def general_kernel(
    n_dp, n_ctx, n_tp, cap,
    ids_ref, codes_ref, tok_hbm, cot_hbm, up_hbm, down_hbm,
    mixed, gtok, gup, gdown,
    tok, cot, up, down, x_send, g_send, x_recv, g_recv, x_all, g_all,
    h_send, a_send, h_recv, a_recv, act, ghid, act_all, ghid_all,
    p_send, q_send, p_recv, q_recv,
    in_sem, xs, xr, gs, gr, hs, hr, as_, ar, cs, cr, ds, dr, ps, pr, qs, qr,
):
    d, c, t = lax.axis_index("dp"), lax.axis_index("ctx"), lax.axis_index("tp")
    n_blocks = n_dp * n_ctx
    me = d * n_ctx + c
    slots = n_ctx * cap

    loads = [
        pltpu.make_async_copy(src, dst, in_sem.at[i])
        for i, (src, dst) in enumerate(
            ((tok_hbm, tok), (cot_hbm, cot), (up_hbm.at[0], up), (down_hbm.at[0], down))
        )
    ]
    for load in loads:
        load.start()

    def block_dev(k):
        b = lax.rem(me + k, n_blocks)
        return b, {"dp": b // n_ctx, "ctx": lax.rem(b, n_ctx)}

    def tp_dev(k):
        j = lax.rem(t + k, n_tp)
        return j, {"tp": j}

    barrier = pltpu.get_barrier_semaphore()
    for k in range(1, n_blocks):
        pl.semaphore_signal(barrier, inc=1, device_id=block_dev(k)[1], device_id_type=MESH)
    for k in range(1, n_tp):
        pl.semaphore_signal(barrier, inc=1, device_id=tp_dev(k)[1], device_id_type=MESH)

    picks, rows = ids_ref.shape
    lane = lax.broadcasted_iota(jnp.int32, (slots, rows), 0)
    lane_e = jnp.zeros((slots, rows), jnp.int32)
    for e in range(1, n_ctx):
        lane_e = lane_e + (lane >= e * cap).astype(jnp.int32)
    lane_s = lane - lane_e * cap
    named = jnp.zeros((slots, rows), jnp.int32)
    code = jnp.zeros((slots, rows), jnp.int32)
    ids, codes = ids_ref[...], codes_ref[...]
    for k in range(picks):
        hit = ids[k : k + 1] == lane_e
        named = jnp.where(hit, 1, named)
        code = jnp.where(hit, codes[k : k + 1], code)
    earlier = (
        lax.broadcasted_iota(jnp.int32, (rows, rows), 0)
        < lax.broadcasted_iota(jnp.int32, (rows, rows), 1)
    )
    rank = dot(named.astype(F32).astype(BF16), earlier.astype(F32).astype(BF16))
    chosen = jnp.where(rank == lane_s.astype(F32), named, 0)
    code = chosen * code
    pick = chosen.astype(F32).astype(BF16)
    high = lax.shift_right_logical(code, 8)
    gate_hi = (high.astype(F32) * (1.0 / 128.0)).astype(BF16)
    gate_lo = ((code - high * 256).astype(F32) * (1.0 / 32768.0)).astype(BF16)

    def groups_dev(g, cc):
        return {"dp": g, "ctx": cc}

    def others(k):
        return range(1 if k == 0 else 0, n_ctx)

    def to(k, m):
        return lax.rem(d + k, n_dp), lax.rem(c + m, n_ctx)

    def spread(send, recv, send_sem, recv_sem, k, back=False):
        for m in others(k):
            g, e = to(k, m)
            src = send.at[g * n_ctx + e] if back else send.at[e]
            pltpu.make_async_remote_copy(
                src, recv.at[me], send_sem.at[k * n_ctx + m], recv_sem.at[me],
                device_id=groups_dev(g, e), device_id_type=MESH,
            ).start()
        if k == 0:
            recv[me] = send[me] if back else send[c]

    def arrived(recv, recv_sem, k):
        g = lax.rem(d + n_dp - k, n_dp)
        for m in others(k):
            e = lax.rem(c + m, n_ctx)
            b = g * n_ctx + e
            pltpu.make_async_remote_copy(
                recv.at[b], recv.at[b], recv_sem.at[b], recv_sem.at[b],
                device_id=groups_dev(g, e), device_id_type=MESH,
            ).wait_recv()
        return g

    def sent(send, send_sem):
        for k in range(n_dp):
            for m in others(k):
                g, e = to(k, m)
                i = k * n_ctx + m
                pltpu.make_async_remote_copy(
                    send.at[0], send.at[0], send_sem.at[i], send_sem.at[i],
                    device_id=groups_dev(g, e), device_id_type=MESH,
                ).wait_send()

    def put_blocks(ref, first, value, count):
        for b in range(count):
            ref[first + b] = value[b * cap : (b + 1) * cap].astype(BF16)

    def take_blocks(ref, first, count):
        return jnp.concatenate(
            [ref[first + b].astype(F32) for b in range(count)], axis=0
        ).astype(BF16)

    def tp_scatter(send, recv, send_sem, recv_sem, k):
        for m in range(1, n_tp):
            j, dev = tp_dev(m)
            pltpu.make_async_remote_copy(
                send.at[k, j], recv.at[k, t], send_sem.at[k, m], recv_sem.at[k, t],
                device_id=dev, device_id_type=MESH,
            ).start()

    def tp_gather(buf, send_sem, recv_sem, k):
        for m in range(1, n_tp):
            j, dev = tp_dev(m)
            pltpu.make_async_remote_copy(
                buf.at[k, t], buf.at[k, t], send_sem.at[k, m], recv_sem.at[k, t],
                device_id=dev, device_id_type=MESH,
            ).start()

    def tp_arrived(buf, recv_sem, k):
        for m in range(1, n_tp):
            j, dev = tp_dev(m)
            pltpu.make_async_remote_copy(
                buf.at[k, j], buf.at[k, j], recv_sem.at[k, j], recv_sem.at[k, j],
                device_id=dev, device_id_type=MESH,
            ).wait_recv()

    def tp_sent(buf, send_sem):
        for k in range(n_dp):
            for m in range(1, n_tp):
                j, dev = tp_dev(m)
                pltpu.make_async_remote_copy(
                    buf.at[k, 0], buf.at[k, 0], send_sem.at[k, m], send_sem.at[k, m],
                    device_id=dev, device_id_type=MESH,
                ).wait_send()

    forth, back = list(range(n_dp)), list(reversed(range(n_dp)))
    loads[0].wait()
    put_blocks(x_send, 0, dot(pick, tok[...]), n_ctx)
    pl.semaphore_wait(barrier, n_blocks - 1 + n_tp - 1)
    for k in forth:
        spread(x_send, x_recv, xs, xr, k)
    loads[1].wait()
    put_blocks(g_send, 0, dot(gate_hi, cot[...]) + dot(gate_lo, cot[...]), n_ctx)
    for k in back:
        spread(g_send, g_recv, gs, gr, k)

    group = slots
    piece = group // n_tp

    def put_pieces(ref, k, value):
        for j in range(n_tp):
            ref[k, j] = value[j * piece : (j + 1) * piece].astype(BF16)

    def total(send, recv, k):
        value = send[k, t].astype(F32)
        for m in range(1, n_tp):
            value = value + recv[k, lax.rem(t + m, n_tp)].astype(F32)
        return value

    loads[2].wait()
    for k in forth:
        g = arrived(x_recv, xr, k)
        x_all[k * group : (k + 1) * group] = take_blocks(x_recv, g * n_ctx, n_ctx)
        put_pieces(h_send, k, dot(x_all[k * group : (k + 1) * group], up[...]))
        tp_scatter(h_send, h_recv, hs, hr, k)
    slopes = [None] * n_dp
    for k in forth:
        tp_arrived(h_recv, hr, k)
        hidden = total(h_send, h_recv, k)
        sigma = 1.0 / (1.0 + jnp.exp(-hidden))
        act[k, t] = (hidden * sigma).astype(BF16)
        tp_gather(act, cs, cr, k)
        slopes[k] = sigma * (1.0 + hidden * (1.0 - sigma))
    loads[3].wait()
    for k in back:
        g = arrived(g_recv, gr, k)
        g_all[k * group : (k + 1) * group] = take_blocks(g_recv, g * n_ctx, n_ctx)
        put_pieces(a_send, k, dot(g_all[k * group : (k + 1) * group], down[...], LAST))
        tp_scatter(a_send, a_recv, as_, ar, k)

    def whole(buf, k):
        return jnp.concatenate([buf[k, j].astype(F32) for j in range(n_tp)], axis=0).astype(BF16)

    def home(k):
        return lax.rem(d + n_dp - k, n_dp) * n_ctx, (n_dp - k) % n_dp

    for k in back:
        rows_k = slice(k * group, (k + 1) * group)
        first, to_k = home(k)
        tp_arrived(act, cr, k)
        act_all[rows_k] = whole(act, k)
        put_blocks(p_send, first, dot(act_all[rows_k], down[...]), n_ctx)
        spread(p_send, p_recv, ps, pr, to_k, back=True)
    for k in back:
        tp_arrived(a_recv, ar, k)
        ghid[k, t] = (total(a_send, a_recv, k) * slopes[k]).astype(BF16)
        tp_gather(ghid, ds, dr, k)
    for k in back:
        rows_k = slice(k * group, (k + 1) * group)
        first, to_k = home(k)
        tp_arrived(ghid, dr, k)
        ghid_all[rows_k] = whole(ghid, k)
        put_blocks(q_send, first, dot(ghid_all[rows_k], up[...], LAST), n_ctx)
        spread(q_send, q_recv, qs, qr, to_k, back=True)

    gdown[0] = dot(act_all[...], g_all[...], FIRST).astype(BF16)
    gup[0] = dot(x_all[...], ghid_all[...], FIRST).astype(BF16)

    for k in back:
        arrived(p_recv, pr, k)
    out = jnp.zeros(mixed.shape, F32)
    for g in range(n_dp):
        got = take_blocks(p_recv, g * n_ctx, n_ctx)
        out = out + dot(gate_hi, got, FIRST) + dot(gate_lo, got, FIRST)
    mixed[...] = out.astype(BF16)
    for k in back:
        arrived(q_recv, qr, k)
    out = jnp.zeros(gtok.shape, F32)
    for g in range(n_dp):
        out = out + dot(pick, take_blocks(q_recv, g * n_ctx, n_ctx), FIRST)
    gtok[...] = out.astype(BF16)

    sent(x_send, xs)
    sent(g_send, gs)
    tp_sent(h_recv, hs)
    tp_sent(a_recv, as_)
    tp_sent(act, cs)
    tp_sent(ghid, ds)
    sent(p_send, ps)
    sent(q_send, qs)


def general_store(*refs):
    sem = refs[-1]
    copies = [
        pltpu.make_async_copy(src, dst, sem.at[i])
        for i, (src, dst) in enumerate(zip(refs[:4], refs[4:8]))
    ]
    for copy in copies:
        copy.start()
    for copy in copies:
        copy.wait()


def general_body(n_dp, n_ctx, n_tp, tokens, expert_ids, gate_codes, up_weight, down_weight, cotangent):
    rows, feats = tokens.shape
    hid = up_weight.shape[2]
    cap = rows // 16
    blocks = n_dp * n_ctx
    total = blocks * cap
    piece = n_ctx * cap // n_tp
    any_ = pl.BlockSpec(memory_space=pl.ANY)
    vmem = pl.BlockSpec(memory_space=pltpu.VMEM)
    dma = pltpu.SemaphoreType.DMA

    def buf(*shape):
        return pltpu.VMEM(shape, BF16)

    tp_sems = [dma((n_dp, n_tp))] * 8
    results = pl.pallas_call(
        functools.partial(general_kernel, n_dp, n_ctx, n_tp, cap),
        out_shape=[
            buf(*a.shape) for a in (tokens, tokens, up_weight, down_weight)
        ],
        in_specs=[vmem, vmem, any_, any_, any_, any_],
        out_specs=[vmem] * 4,
        scratch_shapes=[
            buf(rows, feats), buf(rows, feats), buf(feats, hid), buf(hid, feats),
            buf(n_ctx, cap, feats), buf(n_ctx, cap, feats),
            buf(blocks, cap, feats), buf(blocks, cap, feats),
            buf(total, feats), buf(total, feats),
            buf(n_dp, n_tp, piece, hid), buf(n_dp, n_tp, piece, hid),
            buf(n_dp, n_tp, piece, hid), buf(n_dp, n_tp, piece, hid),
            buf(n_dp, n_tp, piece, hid), buf(n_dp, n_tp, piece, hid),
            buf(total, hid), buf(total, hid),
            buf(blocks, cap, feats), buf(blocks, cap, feats),
            buf(blocks, cap, feats), buf(blocks, cap, feats),
            dma((4,)),
            dma((blocks,)), dma((blocks,)), dma((blocks,)), dma((blocks,)),
            *tp_sems,
            dma((blocks,)), dma((blocks,)), dma((blocks,)), dma((blocks,)),
        ],
        compiler_params=pltpu.CompilerParams(
            collective_id=1, has_side_effects=True, vmem_limit_bytes=58 * 2**20
        ),
        name="general_expert_layer",
    )(expert_ids.T, gate_codes.T, tokens, cotangent, up_weight, down_weight)
    return tuple(
        pl.pallas_call(
            general_store,
            out_shape=[
                jax.ShapeDtypeStruct(a.shape, BF16)
                for a in (tokens, tokens, up_weight, down_weight)
            ],
            in_specs=[vmem] * 4,
            out_specs=[any_] * 4,
            scratch_shapes=[dma((4,))],
            compiler_params=pltpu.CompilerParams(vmem_limit_bytes=2**20),
            name="general_store",
        )(*[pltpu.with_memory_space_constraint(a, pltpu.VMEM) for a in results])
    )


def body(n_dp, n_ctx, n_tp, tokens, expert_ids, gate_codes, up_weight, down_weight, cotangent):
    rows, feats = tokens.shape
    hid = up_weight.shape[2]
    cap = rows // 16
    blocks = n_dp * n_ctx
    total = blocks * cap
    width = hid // n_tp
    near, units, spans = units_of(n_dp, n_ctx)
    picks = expert_ids.shape[1]
    if width % 128:
        return general_body(
            n_dp, n_ctx, n_tp, tokens, expert_ids, gate_codes, up_weight, down_weight, cotangent
        )
    any_ = pl.BlockSpec(memory_space=pl.ANY)
    vmem = pl.BlockSpec(memory_space=pltpu.VMEM)
    dma = pltpu.SemaphoreType.DMA

    def buf(*shape):
        return pltpu.VMEM(shape, BF16)

    block_sems = [dma((blocks,))] * 4
    tp_sems = [dma((len(units), n_tp))] * 8
    results = pl.pallas_call(
        functools.partial(kernel, n_dp, n_ctx, n_tp, cap),
        out_shape=[
            buf(rows, feats), buf(blocks, cap, feats), buf(rows, total),
            buf(*up_weight.shape), buf(*down_weight.shape),
        ],
        in_specs=[any_] * 6,
        out_specs=[vmem] * 5,
        scratch_shapes=[
            pltpu.VMEM((picks, rows), jnp.int32), pltpu.VMEM((picks, rows), jnp.int32),
            buf(rows, feats), buf(rows, feats), buf(feats, hid), buf(hid, feats),
            buf(n_ctx, cap, feats), buf(n_ctx, cap, feats),
            buf(blocks, cap, feats), buf(blocks, cap, feats),
            buf(total, feats), buf(total, feats),
            *[buf(n_tp, total, width)] * 6,
            buf(blocks, cap, feats), buf(blocks, cap, feats), buf(blocks, cap, feats),
            buf(rows, 2 * total),
            dma((6,)),
            *block_sems,
            *tp_sems,
            *block_sems,
        ],
        compiler_params=pltpu.CompilerParams(
            collective_id=0, has_side_effects=True, vmem_limit_bytes=58 * 2**20
        ),
        name="expert_layer",
    )(expert_ids.T, gate_codes.T, tokens, cotangent, up_weight, down_weight)
    return tuple(
        pl.pallas_call(
            functools.partial(store, blocks),
            out_shape=[
                jax.ShapeDtypeStruct(a.shape, BF16)
                for a in (tokens, tokens, up_weight, down_weight)
            ],
            in_specs=[vmem] * 5,
            out_specs=[any_] * 4,
            scratch_shapes=[buf(rows, feats), dma((6,))],
            compiler_params=pltpu.CompilerParams(vmem_limit_bytes=8 * 2**20),
            name="store",
        )(*[pltpu.with_memory_space_constraint(a, pltpu.VMEM) for a in results])
    )


def solution(mesh):
    sizes = [mesh.shape[name] for name in ("dp", "ctx", "tp")]
    return jax.shard_map(
        functools.partial(body, *sizes),
        mesh=mesh,
        in_specs=(
            P(("dp", "ctx"), "tp"),
            P(("dp", "ctx"), None),
            P(("dp", "ctx"), None),
            P("ctx", "tp", "dp"),
            P("ctx", "dp", "tp"),
            P(("dp", "ctx"), "tp"),
        ),
        out_specs=(
            P(("dp", "ctx"), "tp"),
            P(("dp", "ctx"), "tp"),
            P("ctx", "tp", "dp"),
            P("ctx", "dp", "tp"),
        ),
        check_vma=False,
    )
```

```python
import functools

import jax
import jax.numpy as jnp
from jax import lax
from jax.experimental import pallas as pl
from jax.experimental.pallas import tpu as pltpu
from jax.sharding import PartitionSpec as P

MESH = pl.DeviceIdType.MESH
F32 = jnp.float32
BF16 = jnp.bfloat16
FIRST = (((0,), (0,)), ((), ()))
LAST = (((1,), (1,)), ((), ()))
PLAIN = (((1,), (0,)), ((), ()))
CORES = 2


def dot(a, b, how=PLAIN):
    return lax.dot_general(a, b, how, preferred_element_type=F32)


def units_of(n_dp, n_ctx):
    near = CORES if n_ctx % CORES == 0 else 1
    pairs = [(k, m) for k in range(n_dp) for m in range(n_ctx // near)]
    pairs.sort(key=lambda s: (s[0] > 0) + (s[1] > 0))
    return near, pairs


def kernel(
    n_dp, n_ctx, n_tp, cap, spans, send_order, plan,
    ids_hbm, codes_hbm, tok_hbm, cot_hbm, up_hbm, down_hbm,
    mixed, q_recv, pick_t, gup, gdown,
    ids_ref, codes_ref, tok, cot, up, down, x_send, g_send, x_recv, g_recv, x_all, g_all,
    h_send, a_send, h_recv, a_recv, act, ghid, p_send, q_send, p_recv, gate_t,
    in_sem, xs, xr, gs, gr, hs, hr, as_, ar, cs, cr, ds, dr, ps, pr, qs, qr,
):
    near, units = units_of(n_dp, n_ctx)
    d, c, t = lax.axis_index("dp"), lax.axis_index("ctx"), lax.axis_index("tp")
    n_blocks, n_chips = n_dp * n_ctx, n_ctx // near
    me = d * n_ctx + c
    chip, core = c // near, lax.rem(c, near)
    slots = n_ctx * cap
    wide = near * cap
    width = h_send.shape[2]

    loads = [
        pltpu.make_async_copy(src, dst, in_sem.at[i])
        for i, (src, dst) in enumerate((
            (ids_hbm, ids_ref), (codes_hbm, codes_ref), (tok_hbm, tok),
            (cot_hbm, cot), (up_hbm.at[0], up), (down_hbm.at[0], down),
        ))
    ]

    def peer(u, i, sign):
        k, m = units[u]
        g = lax.rem(d + (k if sign > 0 else n_dp - k), n_dp)
        p = lax.rem(chip + (m if sign > 0 else n_chips - m), n_chips)
        e = p * near + lax.rem(core + (i if sign > 0 else near - i), near)
        return g, e, {"dp": g, "ctx": e}

    others = [(u, i) for u in range(len(units)) for i in range(near) if u or i]

    def tp_dev(m):
        j = (t + 1 - 2 * lax.rem(t, 2), lax.rem(t + 2, 4), 3 - t)[m - 1]
        return j, {"tp": j}

    barrier = pltpu.get_barrier_semaphore()
    for u, i in others:
        pl.semaphore_signal(barrier, inc=1, device_id=peer(u, i, 1)[2], device_id_type=MESH)
    for m in range(1, n_tp):
        pl.semaphore_signal(barrier, inc=1, device_id=tp_dev(m)[1], device_id_type=MESH)
    for load in loads[:3]:
        load.start()
    for load in loads[3:]:
        load.start()

    picks, rows = ids_ref.shape
    lane = lax.broadcasted_iota(jnp.int32, (slots, rows), 0)
    lane_e = jnp.zeros((slots, rows), jnp.int32)
    for e in range(1, n_ctx):
        lane_e = lane_e + (lane >= e * cap).astype(jnp.int32)
    lane_s = lane - lane_e * cap
    earlier = (
        lax.broadcasted_iota(jnp.int32, (rows, rows), 0)
        < lax.broadcasted_iota(jnp.int32, (rows, rows), 1)
    ).astype(F32).astype(BF16)
    named = jnp.zeros((slots, rows), jnp.int32)
    code = jnp.zeros((slots, rows), jnp.int32)
    loads[0].wait()
    loads[1].wait()
    ids, codes = ids_ref[...], codes_ref[...]
    for k in range(picks):
        hit = ids[k : k + 1] == lane_e
        named = jnp.where(hit, 1, named)
        code = jnp.where(hit, codes[k : k + 1], code)
    rank = dot(named.astype(F32).astype(BF16), earlier)
    chosen = jnp.where(rank == lane_s.astype(F32), named, 0)
    code = chosen * code
    pick = chosen.astype(F32).astype(BF16)
    high = lax.shift_right_logical(code, 8)
    gate_hi = (high.astype(F32) * (1.0 / 128.0)).astype(BF16)
    gate_lo = ((code - high * 256).astype(F32) * (1.0 / 32768.0)).astype(BF16)

    def remote(src, dst, send, recv, dev):
        return pltpu.make_async_remote_copy(
            src, dst, send, recv, device_id=dev, device_id_type=MESH
        )

    def put_blocks(ref, first, value, count):
        for b in range(count):
            ref[first + b] = value[b * cap : (b + 1) * cap].astype(BF16)

    def join(parts):
        return jnp.concatenate([p.astype(F32) for p in parts], axis=0).astype(BF16)

    def scatter_rows(order, send, recv, send_sem, recv_sem):
        for u in order:
            for i in range(near):
                pos = u * near + i
                if pos:
                    _, e, dev = peer(u, i, 1)
                    remote(
                        send.at[e], recv.at[pos], send_sem.at[pos], recv_sem.at[pos], dev
                    ).start()

    def at(u):
        first, count = spans[u]
        return slice(first * wide, (first + count) * wide)

    def ds_of(u):
        first, count = spans[u]
        return pl.ds(first * wide, count * wide)

    def members(u):
        first, count = spans[u]
        return [(v, i, v * near + i) for v in range(first, first + count) for i in range(near)]

    def collect(u, send, recv, recv_sem, into):
        parts = []
        for v, i, pos in members(u):
            if pos:
                remote(
                    recv.at[pos], recv.at[pos], recv_sem.at[pos], recv_sem.at[pos],
                    peer(v, i, -1)[2],
                ).wait_recv()
                parts.append(recv[pos])
            else:
                parts.append(send[c])
        value = join(parts)
        into[at(u)] = value
        return value

    def cut(u, value, send):
        for j in range(n_tp):
            send[j, at(u)] = value[:, j * width : (j + 1) * width].astype(send.dtype)

    def tp_scatter(u, send, recv, send_sem, recv_sem):
        for m in range(1, n_tp):
            j, dev = tp_dev(m)
            remote(
                send.at[j, ds_of(u)], recv.at[m, ds_of(u)],
                send_sem.at[u, m], recv_sem.at[u, m], dev,
            ).start()

    def tp_total(u, send, recv, recv_sem):
        value = send[t, at(u)].astype(F32)
        for m in range(1, n_tp):
            part = recv.at[m, ds_of(u)]
            sem = recv_sem.at[u, m]
            remote(part, part, sem, sem, tp_dev(m)[1]).wait_recv()
            value = value + recv[m, at(u)].astype(F32)
        return value

    def tp_gather(u, buf, send_sem, recv_sem):
        part = buf.at[t, ds_of(u)]
        for m in range(1, n_tp):
            remote(part, part, send_sem.at[u, m], recv_sem.at[u, m], tp_dev(m)[1]).start()

    def whole(u, buf, recv_sem):
        for m in range(1, n_tp):
            j, dev = tp_dev(m)
            part = buf.at[j, ds_of(u)]
            sem = recv_sem.at[u, m]
            remote(part, part, sem, sem, dev).wait_recv()
        return jnp.concatenate([buf[j, at(u)] for j in range(n_tp)], axis=1)

    def give_back(u, value, send, recv, send_sem, recv_sem):
        put_blocks(send, spans[u][0] * near, value, spans[u][1] * near)
        for v, i, pos in sorted(members(u), key=lambda w: -w[0]):
            if pos:
                remote(
                    send.at[pos], recv.at[me], send_sem.at[pos], recv_sem.at[me],
                    peer(v, i, -1)[2],
                ).start()
            else:
                recv[me] = send[0]

    def returned(recv, recv_sem):
        for u, i in others:
            g, e, dev = peer(u, i, 1)
            b = g * n_ctx + e
            remote(recv.at[b], recv.at[b], recv_sem.at[b], recv_sem.at[b], dev).wait_recv()

    loads[2].wait()
    put_blocks(x_send, 0, dot(pick, tok[...]), n_ctx)
    pl.semaphore_wait(barrier, len(others) + n_tp - 1)
    early = [kind for kind, u in send_order].index("g")
    scatter_rows([u for kind, u in send_order[:early]], x_send, x_recv, xs, xr)
    loads[3].wait()
    put_blocks(g_send, 0, dot(gate_hi, cot[...]) + dot(gate_lo, cot[...]), n_ctx)
    for kind, u in send_order[early:]:
        if kind == "x":
            scatter_rows([u], x_send, x_recv, xs, xr)
        else:
            scatter_rows([u], g_send, g_recv, gs, gr)

    def start_hidden(u):
        value = dot(collect(u, x_send, x_recv, xr, x_all), up[...])
        cut(u, value, h_send)
        tp_scatter(u, h_send, h_recv, hs, hr)

    def start_grad(u):
        value = dot(collect(u, g_send, g_recv, gr, g_all), down[...], LAST)
        cut(u, value, a_send)
        tp_scatter(u, a_send, a_recv, as_, ar)

    slopes = {}

    def activate(u):
        hidden = tp_total(u, h_send, h_recv, hr)
        sigma = 1.0 / (1.0 + jnp.exp(-hidden))
        act[t, at(u)] = (hidden * sigma).astype(BF16)
        slopes[u] = sigma * (1.0 + hidden * (1.0 - sigma))

    def give_act(u):
        tp_gather(u, act, cs, cr)

    def grade(u):
        ghid[t, at(u)] = (tp_total(u, a_send, a_recv, ar) * slopes[u]).astype(BF16)

    def give_ghid(u):
        tp_gather(u, ghid, ds, dr)

    def produce(u):
        value = dot(whole(u, act, cr), down[...])
        give_back(u, value, p_send, p_recv, ps, pr)

    def to_inputs(u):
        value = dot(whole(u, ghid, dr), up[...], LAST)
        give_back(u, value, q_send, q_recv, qs, qr)

    def turn(u):
        twice = jnp.concatenate([pick.astype(F32)] * n_dp, axis=0)
        pick_t[...] = twice.T.astype(BF16)
        gates = jnp.concatenate(
            [gate_hi.astype(F32)] * n_dp + [gate_lo.astype(F32)] * n_dp, axis=0
        )
        gate_t[...] = gates.T.astype(BF16)

    def columns(buf):
        return jnp.concatenate([buf[j] for j in range(n_tp)], axis=1)

    def grad_down(u):
        gdown[0] = dot(columns(act), g_all[...], FIRST).astype(BF16)

    def grad_up(u):
        gup[0] = dot(x_all[...], columns(ghid), FIRST).astype(BF16)

    def mix(u):
        returned(p_recv, pr)
        got = join([p_recv[b] for b in range(n_blocks)])
        half = n_blocks * cap
        mixed[...] = (dot(gate_t[:, :half], got) + dot(gate_t[:, half:], got)).astype(BF16)

    def wait_up(u):
        loads[4].wait()

    def wait_down(u):
        loads[5].wait()

    steps = {
        "up": wait_up, "down": wait_down, "h": start_hidden, "a": start_grad, "turn": turn,
        "act": activate, "ghid": grade, "p": produce, "q": to_inputs,
        "ga": give_act, "gg": give_ghid,
        "gdown": grad_down, "gup": grad_up, "mix": mix,
    }
    for name, u in plan:
        steps[name](u)
    returned(q_recv, qr)

    for u, i in others:
        pos = u * near + i
        for buf, sem in ((x_send, xs), (g_send, gs), (p_send, ps), (q_send, qs)):
            part = buf.at[0]
            remote(part, part, sem.at[pos], sem.at[pos], peer(u, i, 1)[2]).wait_send()
    for u in range(len(spans)):
        for m in range(1, n_tp):
            for buf, sem in ((h_send, hs), (a_send, as_), (act, cs), (ghid, ds)):
                part = buf.at[0, ds_of(u)]
                remote(part, part, sem.at[u, m], sem.at[u, m], tp_dev(m)[1]).wait_send()


STEPS = (
    "up", "h0", "down", "a0", "turn", "h1", "a1", "act0", "ghid0", "h2",
    "act1", "ga1", "a2", "act2", "ga2", "ghid1", "gg1", "p1", "ghid2", "gg2",
    "ga0", "gg0", "p2", "q1", "q2", "p0", "q0", "gdown", "gup", "mix",
)
SENDS = (
    "x1", "x0", "g1", "g0", "x2", "g2",
)


def spans_of(units):
    hops = [(k > 0) + (m > 0) for k, m in units]
    return [(hops.index(h), hops.count(h)) for h in sorted(set(hops))]


def pairs_of(words):
    pairs = []
    for word in words:
        name = word.rstrip("0123456789")
        pairs.append((name, int(word[len(name) :] or 0)))
    return pairs


def plan_of(units):
    spans = spans_of(units)
    sends = [
        (name, u) for name, w in pairs_of(SENDS) for u in range(spans[w][0], sum(spans[w]))[::-1]
    ]
    return spans, sends, pairs_of(STEPS)


def store(n_blocks, mixed, q_recv, pick_t, gup, gdown, mixed_o, gtok_o, gup_o, gdown_o, gtok, sem):
    copies = [
        pltpu.make_async_copy(src, dst, sem.at[i])
        for i, (src, dst) in enumerate(((gup, gup_o), (gdown, gdown_o), (mixed, mixed_o)))
    ]
    for copy in copies:
        copy.start()
    got = jnp.concatenate([q_recv[b].astype(F32) for b in range(n_blocks)], axis=0).astype(BF16)
    rows = gtok.shape[0]
    parts = 3 if rows % 48 == 0 else 1
    step = rows // parts
    for i in range(parts):
        here = slice(i * step, (i + 1) * step)
        gtok[here] = dot(pick_t[here], got).astype(BF16)
        part = pl.ds(i * step, step)
        copy = pltpu.make_async_copy(gtok.at[part], gtok_o.at[part], sem.at[3 + i])
        copy.start()
        copies.append(copy)
    for copy in copies:
        copy.wait()


def general_kernel(
    n_dp, n_ctx, n_tp, cap,
    ids_ref, codes_ref, tok_hbm, cot_hbm, up_hbm, down_hbm,
    mixed, gtok, gup, gdown,
    tok, cot, up, down, x_send, g_send, x_recv, g_recv, x_all, g_all,
    h_send, a_send, h_recv, a_recv, act, ghid, act_all, ghid_all,
    p_send, q_send, p_recv, q_recv,
    in_sem, xs, xr, gs, gr, hs, hr, as_, ar, cs, cr, ds, dr, ps, pr, qs, qr,
):
    d, c, t = lax.axis_index("dp"), lax.axis_index("ctx"), lax.axis_index("tp")
    n_blocks = n_dp * n_ctx
    me = d * n_ctx + c
    slots = n_ctx * cap

    loads = [
        pltpu.make_async_copy(src, dst, in_sem.at[i])
        for i, (src, dst) in enumerate(
            ((tok_hbm, tok), (cot_hbm, cot), (up_hbm.at[0], up), (down_hbm.at[0], down))
        )
    ]
    for load in loads:
        load.start()

    def block_dev(k):
        b = lax.rem(me + k, n_blocks)
        return b, {"dp": b // n_ctx, "ctx": lax.rem(b, n_ctx)}

    def tp_dev(k):
        j = lax.rem(t + k, n_tp)
        return j, {"tp": j}

    barrier = pltpu.get_barrier_semaphore()
    for k in range(1, n_blocks):
        pl.semaphore_signal(barrier, inc=1, device_id=block_dev(k)[1], device_id_type=MESH)
    for k in range(1, n_tp):
        pl.semaphore_signal(barrier, inc=1, device_id=tp_dev(k)[1], device_id_type=MESH)

    picks, rows = ids_ref.shape
    lane = lax.broadcasted_iota(jnp.int32, (slots, rows), 0)
    lane_e = jnp.zeros((slots, rows), jnp.int32)
    for e in range(1, n_ctx):
        lane_e = lane_e + (lane >= e * cap).astype(jnp.int32)
    lane_s = lane - lane_e * cap
    named = jnp.zeros((slots, rows), jnp.int32)
    code = jnp.zeros((slots, rows), jnp.int32)
    ids, codes = ids_ref[...], codes_ref[...]
    for k in range(picks):
        hit = ids[k : k + 1] == lane_e
        named = jnp.where(hit, 1, named)
        code = jnp.where(hit, codes[k : k + 1], code)
    earlier = (
        lax.broadcasted_iota(jnp.int32, (rows, rows), 0)
        < lax.broadcasted_iota(jnp.int32, (rows, rows), 1)
    )
    rank = dot(named.astype(F32).astype(BF16), earlier.astype(F32).astype(BF16))
    chosen = jnp.where(rank == lane_s.astype(F32), named, 0)
    code = chosen * code
    pick = chosen.astype(F32).astype(BF16)
    high = lax.shift_right_logical(code, 8)
    gate_hi = (high.astype(F32) * (1.0 / 128.0)).astype(BF16)
    gate_lo = ((code - high * 256).astype(F32) * (1.0 / 32768.0)).astype(BF16)

    def groups_dev(g, cc):
        return {"dp": g, "ctx": cc}

    def others(k):
        return range(1 if k == 0 else 0, n_ctx)

    def to(k, m):
        return lax.rem(d + k, n_dp), lax.rem(c + m, n_ctx)

    def spread(send, recv, send_sem, recv_sem, k, back=False):
        for m in others(k):
            g, e = to(k, m)
            src = send.at[g * n_ctx + e] if back else send.at[e]
            pltpu.make_async_remote_copy(
                src, recv.at[me], send_sem.at[k * n_ctx + m], recv_sem.at[me],
                device_id=groups_dev(g, e), device_id_type=MESH,
            ).start()
        if k == 0:
            recv[me] = send[me] if back else send[c]

    def arrived(recv, recv_sem, k):
        g = lax.rem(d + n_dp - k, n_dp)
        for m in others(k):
            e = lax.rem(c + m, n_ctx)
            b = g * n_ctx + e
            pltpu.make_async_remote_copy(
                recv.at[b], recv.at[b], recv_sem.at[b], recv_sem.at[b],
                device_id=groups_dev(g, e), device_id_type=MESH,
            ).wait_recv()
        return g

    def sent(send, send_sem):
        for k in range(n_dp):
            for m in others(k):
                g, e = to(k, m)
                i = k * n_ctx + m
                pltpu.make_async_remote_copy(
                    send.at[0], send.at[0], send_sem.at[i], send_sem.at[i],
                    device_id=groups_dev(g, e), device_id_type=MESH,
                ).wait_send()

    def put_blocks(ref, first, value, count):
        for b in range(count):
            ref[first + b] = value[b * cap : (b + 1) * cap].astype(BF16)

    def take_blocks(ref, first, count):
        return jnp.concatenate(
            [ref[first + b].astype(F32) for b in range(count)], axis=0
        ).astype(BF16)

    def tp_scatter(send, recv, send_sem, recv_sem, k):
        for m in range(1, n_tp):
            j, dev = tp_dev(m)
            pltpu.make_async_remote_copy(
                send.at[k, j], recv.at[k, t], send_sem.at[k, m], recv_sem.at[k, t],
                device_id=dev, device_id_type=MESH,
            ).start()

    def tp_gather(buf, send_sem, recv_sem, k):
        for m in range(1, n_tp):
            j, dev = tp_dev(m)
            pltpu.make_async_remote_copy(
                buf.at[k, t], buf.at[k, t], send_sem.at[k, m], recv_sem.at[k, t],
                device_id=dev, device_id_type=MESH,
            ).start()

    def tp_arrived(buf, recv_sem, k):
        for m in range(1, n_tp):
            j, dev = tp_dev(m)
            pltpu.make_async_remote_copy(
                buf.at[k, j], buf.at[k, j], recv_sem.at[k, j], recv_sem.at[k, j],
                device_id=dev, device_id_type=MESH,
            ).wait_recv()

    def tp_sent(buf, send_sem):
        for k in range(n_dp):
            for m in range(1, n_tp):
                j, dev = tp_dev(m)
                pltpu.make_async_remote_copy(
                    buf.at[k, 0], buf.at[k, 0], send_sem.at[k, m], send_sem.at[k, m],
                    device_id=dev, device_id_type=MESH,
                ).wait_send()

    forth, back = list(range(n_dp)), list(reversed(range(n_dp)))
    loads[0].wait()
    put_blocks(x_send, 0, dot(pick, tok[...]), n_ctx)
    pl.semaphore_wait(barrier, n_blocks - 1 + n_tp - 1)
    for k in forth:
        spread(x_send, x_recv, xs, xr, k)
    loads[1].wait()
    put_blocks(g_send, 0, dot(gate_hi, cot[...]) + dot(gate_lo, cot[...]), n_ctx)
    for k in back:
        spread(g_send, g_recv, gs, gr, k)

    group = slots
    piece = group // n_tp

    def put_pieces(ref, k, value):
        for j in range(n_tp):
            ref[k, j] = value[j * piece : (j + 1) * piece].astype(BF16)

    def total(send, recv, k):
        value = send[k, t].astype(F32)
        for m in range(1, n_tp):
            value = value + recv[k, lax.rem(t + m, n_tp)].astype(F32)
        return value

    loads[2].wait()
    for k in forth:
        g = arrived(x_recv, xr, k)
        x_all[k * group : (k + 1) * group] = take_blocks(x_recv, g * n_ctx, n_ctx)
        put_pieces(h_send, k, dot(x_all[k * group : (k + 1) * group], up[...]))
        tp_scatter(h_send, h_recv, hs, hr, k)
    slopes = [None] * n_dp
    for k in forth:
        tp_arrived(h_recv, hr, k)
        hidden = total(h_send, h_recv, k)
        sigma = 1.0 / (1.0 + jnp.exp(-hidden))
        act[k, t] = (hidden * sigma).astype(BF16)
        tp_gather(act, cs, cr, k)
        slopes[k] = sigma * (1.0 + hidden * (1.0 - sigma))
    loads[3].wait()
    for k in back:
        g = arrived(g_recv, gr, k)
        g_all[k * group : (k + 1) * group] = take_blocks(g_recv, g * n_ctx, n_ctx)
        put_pieces(a_send, k, dot(g_all[k * group : (k + 1) * group], down[...], LAST))
        tp_scatter(a_send, a_recv, as_, ar, k)

    def whole(buf, k):
        return jnp.concatenate([buf[k, j].astype(F32) for j in range(n_tp)], axis=0).astype(BF16)

    def home(k):
        return lax.rem(d + n_dp - k, n_dp) * n_ctx, (n_dp - k) % n_dp

    for k in back:
        rows_k = slice(k * group, (k + 1) * group)
        first, to_k = home(k)
        tp_arrived(act, cr, k)
        act_all[rows_k] = whole(act, k)
        put_blocks(p_send, first, dot(act_all[rows_k], down[...]), n_ctx)
        spread(p_send, p_recv, ps, pr, to_k, back=True)
    for k in back:
        tp_arrived(a_recv, ar, k)
        ghid[k, t] = (total(a_send, a_recv, k) * slopes[k]).astype(BF16)
        tp_gather(ghid, ds, dr, k)
    for k in back:
        rows_k = slice(k * group, (k + 1) * group)
        first, to_k = home(k)
        tp_arrived(ghid, dr, k)
        ghid_all[rows_k] = whole(ghid, k)
        put_blocks(q_send, first, dot(ghid_all[rows_k], up[...], LAST), n_ctx)
        spread(q_send, q_recv, qs, qr, to_k, back=True)

    gdown[0] = dot(act_all[...], g_all[...], FIRST).astype(BF16)
    gup[0] = dot(x_all[...], ghid_all[...], FIRST).astype(BF16)

    for k in back:
        arrived(p_recv, pr, k)
    out = jnp.zeros(mixed.shape, F32)
    for g in range(n_dp):
        got = take_blocks(p_recv, g * n_ctx, n_ctx)
        out = out + dot(gate_hi, got, FIRST) + dot(gate_lo, got, FIRST)
    mixed[...] = out.astype(BF16)
    for k in back:
        arrived(q_recv, qr, k)
    out = jnp.zeros(gtok.shape, F32)
    for g in range(n_dp):
        out = out + dot(pick, take_blocks(q_recv, g * n_ctx, n_ctx), FIRST)
    gtok[...] = out.astype(BF16)

    sent(x_send, xs)
    sent(g_send, gs)
    tp_sent(h_recv, hs)
    tp_sent(a_recv, as_)
    tp_sent(act, cs)
    tp_sent(ghid, ds)
    sent(p_send, ps)
    sent(q_send, qs)


def general_store(*refs):
    sem = refs[-1]
    copies = [
        pltpu.make_async_copy(src, dst, sem.at[i])
        for i, (src, dst) in enumerate(zip(refs[:4], refs[4:8]))
    ]
    for copy in copies:
        copy.start()
    for copy in copies:
        copy.wait()


def general_body(n_dp, n_ctx, n_tp, tokens, expert_ids, gate_codes, up_weight, down_weight, cotangent):
    rows, feats = tokens.shape
    hid = up_weight.shape[2]
    cap = rows // 16
    blocks = n_dp * n_ctx
    total = blocks * cap
    piece = n_ctx * cap // n_tp
    any_ = pl.BlockSpec(memory_space=pl.ANY)
    vmem = pl.BlockSpec(memory_space=pltpu.VMEM)
    dma = pltpu.SemaphoreType.DMA

    def buf(*shape):
        return pltpu.VMEM(shape, BF16)

    tp_sems = [dma((n_dp, n_tp))] * 8
    results = pl.pallas_call(
        functools.partial(general_kernel, n_dp, n_ctx, n_tp, cap),
        out_shape=[
            buf(*a.shape) for a in (tokens, tokens, up_weight, down_weight)
        ],
        in_specs=[vmem, vmem, any_, any_, any_, any_],
        out_specs=[vmem] * 4,
        scratch_shapes=[
            buf(rows, feats), buf(rows, feats), buf(feats, hid), buf(hid, feats),
            buf(n_ctx, cap, feats), buf(n_ctx, cap, feats),
            buf(blocks, cap, feats), buf(blocks, cap, feats),
            buf(total, feats), buf(total, feats),
            buf(n_dp, n_tp, piece, hid), buf(n_dp, n_tp, piece, hid),
            buf(n_dp, n_tp, piece, hid), buf(n_dp, n_tp, piece, hid),
            buf(n_dp, n_tp, piece, hid), buf(n_dp, n_tp, piece, hid),
            buf(total, hid), buf(total, hid),
            buf(blocks, cap, feats), buf(blocks, cap, feats),
            buf(blocks, cap, feats), buf(blocks, cap, feats),
            dma((4,)),
            dma((blocks,)), dma((blocks,)), dma((blocks,)), dma((blocks,)),
            *tp_sems,
            dma((blocks,)), dma((blocks,)), dma((blocks,)), dma((blocks,)),
        ],
        compiler_params=pltpu.CompilerParams(
            collective_id=1, has_side_effects=True, vmem_limit_bytes=58 * 2**20
        ),
        name="general_expert_layer",
    )(expert_ids.T, gate_codes.T, tokens, cotangent, up_weight, down_weight)
    return tuple(
        pl.pallas_call(
            general_store,
            out_shape=[
                jax.ShapeDtypeStruct(a.shape, BF16)
                for a in (tokens, tokens, up_weight, down_weight)
            ],
            in_specs=[vmem] * 4,
            out_specs=[any_] * 4,
            scratch_shapes=[dma((4,))],
            compiler_params=pltpu.CompilerParams(vmem_limit_bytes=2**20),
            name="general_store",
        )(*[pltpu.with_memory_space_constraint(a, pltpu.VMEM) for a in results])
    )


def body(n_dp, n_ctx, n_tp, tokens, expert_ids, gate_codes, up_weight, down_weight, cotangent):
    rows, feats = tokens.shape
    hid = up_weight.shape[2]
    cap = rows // 16
    blocks = n_dp * n_ctx
    total = blocks * cap
    width = hid // n_tp
    near, units = units_of(n_dp, n_ctx)
    picks = expert_ids.shape[1]
    if width % 128 or n_tp != 4 or len(spans_of(units)) != 3 or near != CORES:
        return general_body(
            n_dp, n_ctx, n_tp, tokens, expert_ids, gate_codes, up_weight, down_weight, cotangent
        )
    any_ = pl.BlockSpec(memory_space=pl.ANY)
    vmem = pl.BlockSpec(memory_space=pltpu.VMEM)
    dma = pltpu.SemaphoreType.DMA

    def buf(*shape):
        return pltpu.VMEM(shape, BF16)

    block_sems = [dma((blocks,))] * 4
    tp_sems = [dma((len(units), n_tp))] * 8
    results = pl.pallas_call(
        functools.partial(kernel, n_dp, n_ctx, n_tp, cap, *plan_of(units)),
        out_shape=[
            buf(rows, feats), buf(blocks, cap, feats), buf(rows, total),
            buf(*up_weight.shape), buf(*down_weight.shape),
        ],
        in_specs=[any_] * 6,
        out_specs=[vmem] * 5,
        scratch_shapes=[
            pltpu.VMEM((picks, rows), jnp.int32), pltpu.VMEM((picks, rows), jnp.int32),
            buf(rows, feats), buf(rows, feats), buf(feats, hid), buf(hid, feats),
            buf(n_ctx, cap, feats), buf(n_ctx, cap, feats),
            buf(blocks, cap, feats), buf(blocks, cap, feats),
            buf(total, feats), buf(total, feats),
            *[buf(n_tp, total, width)] * 6,
            buf(blocks, cap, feats), buf(blocks, cap, feats), buf(blocks, cap, feats),
            buf(rows, 2 * total),
            dma((6,)),
            *block_sems,
            *tp_sems,
            *block_sems,
        ],
        compiler_params=pltpu.CompilerParams(
            collective_id=0, has_side_effects=True, vmem_limit_bytes=58 * 2**20
        ),
        name="expert_layer",
    )(expert_ids.T, gate_codes.T, tokens, cotangent, up_weight, down_weight)
    return tuple(
        pl.pallas_call(
            functools.partial(store, blocks),
            out_shape=[
                jax.ShapeDtypeStruct(a.shape, BF16)
                for a in (tokens, tokens, up_weight, down_weight)
            ],
            in_specs=[vmem] * 5,
            out_specs=[any_] * 4,
            scratch_shapes=[buf(rows, feats), dma((6,))],
            compiler_params=pltpu.CompilerParams(vmem_limit_bytes=8 * 2**20),
            name="store",
        )(*[pltpu.with_memory_space_constraint(a, pltpu.VMEM) for a in results])
    )


def solution(mesh):
    sizes = [mesh.shape[name] for name in ("dp", "ctx", "tp")]
    return jax.shard_map(
        functools.partial(body, *sizes),
        mesh=mesh,
        in_specs=(
            P(("dp", "ctx"), "tp"),
            P(("dp", "ctx"), None),
            P(("dp", "ctx"), None),
            P("ctx", "tp", "dp"),
            P("ctx", "dp", "tp"),
            P(("dp", "ctx"), "tp"),
        ),
        out_specs=(
            P(("dp", "ctx"), "tp"),
            P(("dp", "ctx"), "tp"),
            P("ctx", "tp", "dp"),
            P("ctx", "dp", "tp"),
        ),
        check_vma=False,
    )
```

```python
import functools

import jax
import jax.numpy as jnp
from jax import lax
from jax.experimental import pallas as pl
from jax.experimental.pallas import tpu as pltpu
from jax.sharding import PartitionSpec as P

MESH = pl.DeviceIdType.MESH
F32 = jnp.float32
BF16 = jnp.bfloat16
FIRST = (((0,), (0,)), ((), ()))
LAST = (((1,), (1,)), ((), ()))
PLAIN = (((1,), (0,)), ((), ()))
CORES = 2


def dot(a, b, how=PLAIN):
    return lax.dot_general(a, b, how, preferred_element_type=F32)


def units_of(n_dp, n_ctx):
    near = CORES if n_ctx % CORES == 0 else 1
    pairs = [(k, m) for k in range(n_dp) for m in range(n_ctx // near)]
    pairs.sort(key=lambda s: (s[0] > 0) + (s[1] > 0))
    return near, pairs


def kernel(
    n_dp, n_ctx, n_tp, cap, spans, send_order, plan,
    ids_hbm, codes_hbm, tok_hbm, cot_hbm, up_hbm, down_hbm,
    mixed, q_recv, pick_t, gup, gdown,
    ids_ref, codes_ref, tok, cot, up, down, x_send, g_send, x_recv, g_recv, x_all, g_all,
    h_send, a_send, h_recv, a_recv, act, ghid, p_send, q_send, p_recv, gate_t, up_t, down_t,
    in_sem, xs, xr, gs, gr, hs, hr, as_, ar, cs, cr, ds, dr, ps, pr, qs, qr,
):
    near, units = units_of(n_dp, n_ctx)
    d, c, t = lax.axis_index("dp"), lax.axis_index("ctx"), lax.axis_index("tp")
    n_blocks, n_chips = n_dp * n_ctx, n_ctx // near
    me = d * n_ctx + c
    chip, core = c // near, lax.rem(c, near)
    slots = n_ctx * cap
    wide = near * cap
    width = h_send.shape[2]

    loads = [
        pltpu.make_async_copy(src, dst, in_sem.at[i])
        for i, (src, dst) in enumerate((
            (ids_hbm, ids_ref), (codes_hbm, codes_ref), (tok_hbm, tok),
            (cot_hbm, cot), (up_hbm.at[0], up), (down_hbm.at[0], down),
        ))
    ]

    def peer(u, i, sign):
        k, m = units[u]
        g = lax.rem(d + (k if sign > 0 else n_dp - k), n_dp)
        p = lax.rem(chip + (m if sign > 0 else n_chips - m), n_chips)
        e = p * near + lax.rem(core + (i if sign > 0 else near - i), near)
        return g, e, {"dp": g, "ctx": e}

    others = [(u, i) for u in range(len(units)) for i in range(near) if u or i]

    def tp_dev(m):
        j = (t + 1 - 2 * lax.rem(t, 2), lax.rem(t + 2, 4), 3 - t)[m - 1]
        return j, {"tp": j}

    barrier = pltpu.get_barrier_semaphore()
    for u, i in others:
        pl.semaphore_signal(barrier, inc=1, device_id=peer(u, i, 1)[2], device_id_type=MESH)
    for m in range(1, n_tp):
        pl.semaphore_signal(barrier, inc=1, device_id=tp_dev(m)[1], device_id_type=MESH)
    for load in loads[:3]:
        load.start()
    for load in loads[3:]:
        load.start()

    picks, rows = ids_ref.shape
    lane = lax.broadcasted_iota(jnp.int32, (slots, rows), 0)
    lane_e = jnp.zeros((slots, rows), jnp.int32)
    for e in range(1, n_ctx):
        lane_e = lane_e + (lane >= e * cap).astype(jnp.int32)
    lane_s = lane - lane_e * cap
    earlier = (
        lax.broadcasted_iota(jnp.int32, (rows, rows), 0)
        < lax.broadcasted_iota(jnp.int32, (rows, rows), 1)
    ).astype(F32).astype(BF16)
    named = jnp.zeros((slots, rows), jnp.int32)
    code = jnp.zeros((slots, rows), jnp.int32)
    loads[0].wait()
    loads[1].wait()
    ids, codes = ids_ref[...], codes_ref[...]
    for k in range(picks):
        hit = ids[k : k + 1] == lane_e
        named = jnp.where(hit, 1, named)
        code = jnp.where(hit, codes[k : k + 1], code)
    rank = dot(named.astype(F32).astype(BF16), earlier)
    chosen = jnp.where(rank == lane_s.astype(F32), named, 0)
    code = chosen * code
    pick = chosen.astype(F32).astype(BF16)
    gate = jnp.sum(code.astype(F32), axis=1, keepdims=True) * (1.0 / 32768.0)

    def remote(src, dst, send, recv, dev):
        return pltpu.make_async_remote_copy(
            src, dst, send, recv, device_id=dev, device_id_type=MESH
        )

    def put_blocks(ref, first, value, count):
        for b in range(count):
            ref[first + b] = value[b * cap : (b + 1) * cap].astype(BF16)

    def join(parts):
        return jnp.concatenate([p.astype(F32) for p in parts], axis=0).astype(BF16)

    def scatter_rows(order, send, recv, send_sem, recv_sem):
        for u in order:
            for i in range(near):
                pos = u * near + i
                if pos:
                    _, e, dev = peer(u, i, 1)
                    remote(
                        send.at[e], recv.at[pos], send_sem.at[pos], recv_sem.at[pos], dev
                    ).start()

    def at(u):
        first, count = spans[u]
        return slice(first * wide, (first + count) * wide)

    def ds_of(u):
        first, count = spans[u]
        return pl.ds(first * wide, count * wide)

    def members(u):
        first, count = spans[u]
        return [(v, i, v * near + i) for v in range(first, first + count) for i in range(near)]

    def collect(u, send, recv, recv_sem, into):
        parts = []
        for v, i, pos in members(u):
            if pos:
                remote(
                    recv.at[pos], recv.at[pos], recv_sem.at[pos], recv_sem.at[pos],
                    peer(v, i, -1)[2],
                ).wait_recv()
                parts.append(recv[pos])
            else:
                parts.append(send[c])
        value = join(parts)
        into[at(u)] = value
        return value

    def cut(u, value, send):
        for j in range(n_tp):
            send[j, at(u)] = value[:, j * width : (j + 1) * width].astype(send.dtype)

    def tp_scatter(u, send, recv, send_sem, recv_sem):
        for m in range(1, n_tp):
            j, dev = tp_dev(m)
            remote(
                send.at[j, ds_of(u)], recv.at[m, ds_of(u)],
                send_sem.at[u, m], recv_sem.at[u, m], dev,
            ).start()

    def tp_total(u, send, recv, recv_sem):
        value = send[t, at(u)].astype(F32)
        for m in range(1, n_tp):
            part = recv.at[m, ds_of(u)]
            sem = recv_sem.at[u, m]
            remote(part, part, sem, sem, tp_dev(m)[1]).wait_recv()
            value = value + recv[m, at(u)].astype(F32)
        return value

    def tp_gather(u, buf, send_sem, recv_sem):
        part = buf.at[t, ds_of(u)]
        for m in range(1, n_tp):
            remote(part, part, send_sem.at[u, m], recv_sem.at[u, m], tp_dev(m)[1]).start()

    def whole(u, buf, recv_sem):
        for m in range(1, n_tp):
            j, dev = tp_dev(m)
            part = buf.at[j, ds_of(u)]
            sem = recv_sem.at[u, m]
            remote(part, part, sem, sem, dev).wait_recv()
        return jnp.concatenate([buf[j, at(u)] for j in range(n_tp)], axis=1)

    def give_back(u, value, send, recv, send_sem, recv_sem):
        put_blocks(send, spans[u][0] * near, value, spans[u][1] * near)
        for v, i, pos in sorted(members(u), key=lambda w: -w[0]):
            if pos:
                remote(
                    send.at[pos], recv.at[me], send_sem.at[pos], recv_sem.at[me],
                    peer(v, i, -1)[2],
                ).start()
            else:
                recv[me] = send[0]

    def returned(recv, recv_sem):
        for u, i in others:
            g, e, dev = peer(u, i, 1)
            b = g * n_ctx + e
            remote(recv.at[b], recv.at[b], recv_sem.at[b], recv_sem.at[b], dev).wait_recv()

    loads[2].wait()
    put_blocks(x_send, 0, dot(pick, tok[...]), n_ctx)
    pl.semaphore_wait(barrier, len(others) + n_tp - 1)
    early = [kind for kind, u in send_order].index("g")
    scatter_rows([u for kind, u in send_order[:early]], x_send, x_recv, xs, xr)
    loads[3].wait()
    put_blocks(g_send, 0, dot(pick, cot[...]) * gate, n_ctx)
    for kind, u in send_order[early:]:
        if kind == "x":
            scatter_rows([u], x_send, x_recv, xs, xr)
        else:
            scatter_rows([u], g_send, g_recv, gs, gr)

    def start_hidden(u):
        value = dot(collect(u, x_send, x_recv, xr, x_all), up[...])
        cut(u, value, h_send)
        tp_scatter(u, h_send, h_recv, hs, hr)

    def start_grad(u):
        g = collect(u, g_send, g_recv, gr, g_all)
        value = dot(g, down_t[...]) if u else dot(g, down[...], LAST)
        cut(u, value, a_send)
        tp_scatter(u, a_send, a_recv, as_, ar)

    slopes = {}

    def activate(u):
        hidden = tp_total(u, h_send, h_recv, hr)
        sigma = 1.0 / (1.0 + jnp.exp(-hidden))
        act[t, at(u)] = (hidden * sigma).astype(BF16)
        slopes[u] = sigma * (1.0 + hidden * (1.0 - sigma))

    def give_act(u):
        tp_gather(u, act, cs, cr)

    def grade(u):
        ghid[t, at(u)] = (tp_total(u, a_send, a_recv, ar) * slopes[u]).astype(BF16)

    def give_ghid(u):
        tp_gather(u, ghid, ds, dr)

    def produce(u):
        value = dot(whole(u, act, cr), down[...])
        give_back(u, value, p_send, p_recv, ps, pr)

    def to_inputs(u):
        value = dot(whole(u, ghid, dr), up_t[...])
        give_back(u, value, q_send, q_recv, qs, qr)

    def turn(u):
        high = lax.shift_right_logical(code, 8)
        gate_hi = (high.astype(F32) * (1.0 / 128.0)).astype(BF16)
        gate_lo = ((code - high * 256).astype(F32) * (1.0 / 32768.0)).astype(BF16)
        twice = jnp.concatenate([pick.astype(F32)] * n_dp, axis=0)
        pick_t[...] = twice.T.astype(BF16)
        gates = jnp.concatenate(
            [gate_hi.astype(F32)] * n_dp + [gate_lo.astype(F32)] * n_dp, axis=0
        )
        gate_t[...] = gates.T.astype(BF16)
        up_t[...] = up[...].T
        down_t[...] = down[...].T

    def columns(buf):
        return jnp.concatenate([buf[j] for j in range(n_tp)], axis=1)

    def grad_down(u):
        gdown[0] = dot(columns(act), g_all[...], FIRST).astype(BF16)

    def grad_up(u):
        gup[0] = dot(x_all[...], columns(ghid), FIRST).astype(BF16)

    def mix(u):
        returned(p_recv, pr)
        got = join([p_recv[b] for b in range(n_blocks)])
        half = n_blocks * cap
        mixed[...] = (dot(gate_t[:, :half], got) + dot(gate_t[:, half:], got)).astype(BF16)

    def wait_up(u):
        loads[4].wait()

    def wait_down(u):
        loads[5].wait()

    def sent(u):
        for v, i in others:
            pos = v * near + i
            for buf, sem in ((x_send, xs), (g_send, gs), (p_send, ps)):
                part = buf.at[0]
                remote(part, part, sem.at[pos], sem.at[pos], peer(v, i, 1)[2]).wait_send()
        for u in range(len(spans)):
            for m in range(1, n_tp):
                for buf, sem in ((h_send, hs), (a_send, as_), (act, cs), (ghid, ds)):
                    part = buf.at[0, ds_of(u)]
                    remote(part, part, sem.at[u, m], sem.at[u, m], tp_dev(m)[1]).wait_send()

    steps = {
        "sent": sent,
        "up": wait_up, "down": wait_down, "h": start_hidden, "a": start_grad, "turn": turn,
        "act": activate, "ghid": grade, "p": produce, "q": to_inputs,
        "ga": give_act, "gg": give_ghid,
        "gdown": grad_down, "gup": grad_up, "mix": mix,
    }
    for name, u in plan:
        steps[name](u)
    returned(q_recv, qr)

    for v, i in others:
        pos = v * near + i
        part = q_send.at[0]
        remote(part, part, qs.at[pos], qs.at[pos], peer(v, i, 1)[2]).wait_send()


STEPS = (
    "up", "h0", "down", "a0", "turn", "h1", "a1", "act0", "ghid0", "h2",
    "act1", "ga1", "a2", "act2", "ga2", "ghid1", "gg1", "p1", "ghid2", "gg2",
    "ga0", "gg0", "p2", "q1", "q2", "p0", "q0", "sent", "gdown", "gup",
    "mix",
)
SENDS = (
    "x1", "x0", "g1", "g0", "x2", "g2",
)


def spans_of(units):
    hops = [(k > 0) + (m > 0) for k, m in units]
    return [(hops.index(h), hops.count(h)) for h in sorted(set(hops))]


def pairs_of(words):
    pairs = []
    for word in words:
        name = word.rstrip("0123456789")
        pairs.append((name, int(word[len(name) :] or 0)))
    return pairs


def plan_of(units):
    spans = spans_of(units)
    sends = [
        (name, u) for name, w in pairs_of(SENDS) for u in range(spans[w][0], sum(spans[w]))[::-1]
    ]
    return spans, sends, pairs_of(STEPS)


def store(n_blocks, mixed, q_recv, pick_t, gup, gdown, mixed_o, gtok_o, gup_o, gdown_o, gtok, sem):
    copies = [
        pltpu.make_async_copy(src, dst, sem.at[i])
        for i, (src, dst) in enumerate(((gup, gup_o), (gdown, gdown_o), (mixed, mixed_o)))
    ]
    for copy in copies:
        copy.start()
    got = jnp.concatenate([q_recv[b].astype(F32) for b in range(n_blocks)], axis=0).astype(BF16)
    rows = gtok.shape[0]
    parts = 3 if rows % 48 == 0 else 1
    step = rows // parts
    for i in range(parts):
        here = slice(i * step, (i + 1) * step)
        gtok[here] = dot(pick_t[here], got).astype(BF16)
        part = pl.ds(i * step, step)
        copy = pltpu.make_async_copy(gtok.at[part], gtok_o.at[part], sem.at[3 + i])
        copy.start()
        copies.append(copy)
    for copy in copies:
        copy.wait()


def general_kernel(
    n_dp, n_ctx, n_tp, cap,
    ids_ref, codes_ref, tok_hbm, cot_hbm, up_hbm, down_hbm,
    mixed, gtok, gup, gdown,
    tok, cot, up, down, x_send, g_send, x_recv, g_recv, x_all, g_all,
    h_send, a_send, h_recv, a_recv, act, ghid, act_all, ghid_all,
    p_send, q_send, p_recv, q_recv,
    in_sem, xs, xr, gs, gr, hs, hr, as_, ar, cs, cr, ds, dr, ps, pr, qs, qr,
):
    d, c, t = lax.axis_index("dp"), lax.axis_index("ctx"), lax.axis_index("tp")
    n_blocks = n_dp * n_ctx
    me = d * n_ctx + c
    slots = n_ctx * cap

    loads = [
        pltpu.make_async_copy(src, dst, in_sem.at[i])
        for i, (src, dst) in enumerate(
            ((tok_hbm, tok), (cot_hbm, cot), (up_hbm.at[0], up), (down_hbm.at[0], down))
        )
    ]
    for load in loads:
        load.start()

    def block_dev(k):
        b = lax.rem(me + k, n_blocks)
        return b, {"dp": b // n_ctx, "ctx": lax.rem(b, n_ctx)}

    def tp_dev(k):
        j = lax.rem(t + k, n_tp)
        return j, {"tp": j}

    barrier = pltpu.get_barrier_semaphore()
    for k in range(1, n_blocks):
        pl.semaphore_signal(barrier, inc=1, device_id=block_dev(k)[1], device_id_type=MESH)
    for k in range(1, n_tp):
        pl.semaphore_signal(barrier, inc=1, device_id=tp_dev(k)[1], device_id_type=MESH)

    picks, rows = ids_ref.shape
    lane = lax.broadcasted_iota(jnp.int32, (slots, rows), 0)
    lane_e = jnp.zeros((slots, rows), jnp.int32)
    for e in range(1, n_ctx):
        lane_e = lane_e + (lane >= e * cap).astype(jnp.int32)
    lane_s = lane - lane_e * cap
    named = jnp.zeros((slots, rows), jnp.int32)
    code = jnp.zeros((slots, rows), jnp.int32)
    ids, codes = ids_ref[...], codes_ref[...]
    for k in range(picks):
        hit = ids[k : k + 1] == lane_e
        named = jnp.where(hit, 1, named)
        code = jnp.where(hit, codes[k : k + 1], code)
    earlier = (
        lax.broadcasted_iota(jnp.int32, (rows, rows), 0)
        < lax.broadcasted_iota(jnp.int32, (rows, rows), 1)
    )
    rank = dot(named.astype(F32).astype(BF16), earlier.astype(F32).astype(BF16))
    chosen = jnp.where(rank == lane_s.astype(F32), named, 0)
    code = chosen * code
    pick = chosen.astype(F32).astype(BF16)
    high = lax.shift_right_logical(code, 8)
    gate_hi = (high.astype(F32) * (1.0 / 128.0)).astype(BF16)
    gate_lo = ((code - high * 256).astype(F32) * (1.0 / 32768.0)).astype(BF16)

    def groups_dev(g, cc):
        return {"dp": g, "ctx": cc}

    def others(k):
        return range(1 if k == 0 else 0, n_ctx)

    def to(k, m):
        return lax.rem(d + k, n_dp), lax.rem(c + m, n_ctx)

    def spread(send, recv, send_sem, recv_sem, k, back=False):
        for m in others(k):
            g, e = to(k, m)
            src = send.at[g * n_ctx + e] if back else send.at[e]
            pltpu.make_async_remote_copy(
                src, recv.at[me], send_sem.at[k * n_ctx + m], recv_sem.at[me],
                device_id=groups_dev(g, e), device_id_type=MESH,
            ).start()
        if k == 0:
            recv[me] = send[me] if back else send[c]

    def arrived(recv, recv_sem, k):
        g = lax.rem(d + n_dp - k, n_dp)
        for m in others(k):
            e = lax.rem(c + m, n_ctx)
            b = g * n_ctx + e
            pltpu.make_async_remote_copy(
                recv.at[b], recv.at[b], recv_sem.at[b], recv_sem.at[b],
                device_id=groups_dev(g, e), device_id_type=MESH,
            ).wait_recv()
        return g

    def sent(send, send_sem):
        for k in range(n_dp):
            for m in others(k):
                g, e = to(k, m)
                i = k * n_ctx + m
                pltpu.make_async_remote_copy(
                    send.at[0], send.at[0], send_sem.at[i], send_sem.at[i],
                    device_id=groups_dev(g, e), device_id_type=MESH,
                ).wait_send()

    def put_blocks(ref, first, value, count):
        for b in range(count):
            ref[first + b] = value[b * cap : (b + 1) * cap].astype(BF16)

    def take_blocks(ref, first, count):
        return jnp.concatenate(
            [ref[first + b].astype(F32) for b in range(count)], axis=0
        ).astype(BF16)

    def tp_scatter(send, recv, send_sem, recv_sem, k):
        for m in range(1, n_tp):
            j, dev = tp_dev(m)
            pltpu.make_async_remote_copy(
                send.at[k, j], recv.at[k, t], send_sem.at[k, m], recv_sem.at[k, t],
                device_id=dev, device_id_type=MESH,
            ).start()

    def tp_gather(buf, send_sem, recv_sem, k):
        for m in range(1, n_tp):
            j, dev = tp_dev(m)
            pltpu.make_async_remote_copy(
                buf.at[k, t], buf.at[k, t], send_sem.at[k, m], recv_sem.at[k, t],
                device_id=dev, device_id_type=MESH,
            ).start()

    def tp_arrived(buf, recv_sem, k):
        for m in range(1, n_tp):
            j, dev = tp_dev(m)
            pltpu.make_async_remote_copy(
                buf.at[k, j], buf.at[k, j], recv_sem.at[k, j], recv_sem.at[k, j],
                device_id=dev, device_id_type=MESH,
            ).wait_recv()

    def tp_sent(buf, send_sem):
        for k in range(n_dp):
            for m in range(1, n_tp):
                j, dev = tp_dev(m)
                pltpu.make_async_remote_copy(
                    buf.at[k, 0], buf.at[k, 0], send_sem.at[k, m], send_sem.at[k, m],
                    device_id=dev, device_id_type=MESH,
                ).wait_send()

    forth, back = list(range(n_dp)), list(reversed(range(n_dp)))
    loads[0].wait()
    put_blocks(x_send, 0, dot(pick, tok[...]), n_ctx)
    pl.semaphore_wait(barrier, n_blocks - 1 + n_tp - 1)
    for k in forth:
        spread(x_send, x_recv, xs, xr, k)
    loads[1].wait()
    put_blocks(g_send, 0, dot(gate_hi, cot[...]) + dot(gate_lo, cot[...]), n_ctx)
    for k in back:
        spread(g_send, g_recv, gs, gr, k)

    group = slots
    piece = group // n_tp

    def put_pieces(ref, k, value):
        for j in range(n_tp):
            ref[k, j] = value[j * piece : (j + 1) * piece].astype(BF16)

    def total(send, recv, k):
        value = send[k, t].astype(F32)
        for m in range(1, n_tp):
            value = value + recv[k, lax.rem(t + m, n_tp)].astype(F32)
        return value

    loads[2].wait()
    for k in forth:
        g = arrived(x_recv, xr, k)
        x_all[k * group : (k + 1) * group] = take_blocks(x_recv, g * n_ctx, n_ctx)
        put_pieces(h_send, k, dot(x_all[k * group : (k + 1) * group], up[...]))
        tp_scatter(h_send, h_recv, hs, hr, k)
    slopes = [None] * n_dp
    for k in forth:
        tp_arrived(h_recv, hr, k)
        hidden = total(h_send, h_recv, k)
        sigma = 1.0 / (1.0 + jnp.exp(-hidden))
        act[k, t] = (hidden * sigma).astype(BF16)
        tp_gather(act, cs, cr, k)
        slopes[k] = sigma * (1.0 + hidden * (1.0 - sigma))
    loads[3].wait()
    for k in back:
        g = arrived(g_recv, gr, k)
        g_all[k * group : (k + 1) * group] = take_blocks(g_recv, g * n_ctx, n_ctx)
        put_pieces(a_send, k, dot(g_all[k * group : (k + 1) * group], down[...], LAST))
        tp_scatter(a_send, a_recv, as_, ar, k)

    def whole(buf, k):
        return jnp.concatenate([buf[k, j].astype(F32) for j in range(n_tp)], axis=0).astype(BF16)

    def home(k):
        return lax.rem(d + n_dp - k, n_dp) * n_ctx, (n_dp - k) % n_dp

    for k in back:
        rows_k = slice(k * group, (k + 1) * group)
        first, to_k = home(k)
        tp_arrived(act, cr, k)
        act_all[rows_k] = whole(act, k)
        put_blocks(p_send, first, dot(act_all[rows_k], down[...]), n_ctx)
        spread(p_send, p_recv, ps, pr, to_k, back=True)
    for k in back:
        tp_arrived(a_recv, ar, k)
        ghid[k, t] = (total(a_send, a_recv, k) * slopes[k]).astype(BF16)
        tp_gather(ghid, ds, dr, k)
    for k in back:
        rows_k = slice(k * group, (k + 1) * group)
        first, to_k = home(k)
        tp_arrived(ghid, dr, k)
        ghid_all[rows_k] = whole(ghid, k)
        put_blocks(q_send, first, dot(ghid_all[rows_k], up[...], LAST), n_ctx)
        spread(q_send, q_recv, qs, qr, to_k, back=True)

    gdown[0] = dot(act_all[...], g_all[...], FIRST).astype(BF16)
    gup[0] = dot(x_all[...], ghid_all[...], FIRST).astype(BF16)

    for k in back:
        arrived(p_recv, pr, k)
    out = jnp.zeros(mixed.shape, F32)
    for g in range(n_dp):
        got = take_blocks(p_recv, g * n_ctx, n_ctx)
        out = out + dot(gate_hi, got, FIRST) + dot(gate_lo, got, FIRST)
    mixed[...] = out.astype(BF16)
    for k in back:
        arrived(q_recv, qr, k)
    out = jnp.zeros(gtok.shape, F32)
    for g in range(n_dp):
        out = out + dot(pick, take_blocks(q_recv, g * n_ctx, n_ctx), FIRST)
    gtok[...] = out.astype(BF16)

    sent(x_send, xs)
    sent(g_send, gs)
    tp_sent(h_recv, hs)
    tp_sent(a_recv, as_)
    tp_sent(act, cs)
    tp_sent(ghid, ds)
    sent(p_send, ps)
    sent(q_send, qs)


def general_store(*refs):
    sem = refs[-1]
    copies = [
        pltpu.make_async_copy(src, dst, sem.at[i])
        for i, (src, dst) in enumerate(zip(refs[:4], refs[4:8]))
    ]
    for copy in copies:
        copy.start()
    for copy in copies:
        copy.wait()


def general_body(n_dp, n_ctx, n_tp, tokens, expert_ids, gate_codes, up_weight, down_weight, cotangent):
    rows, feats = tokens.shape
    hid = up_weight.shape[2]
    cap = rows // 16
    blocks = n_dp * n_ctx
    total = blocks * cap
    piece = n_ctx * cap // n_tp
    any_ = pl.BlockSpec(memory_space=pl.ANY)
    vmem = pl.BlockSpec(memory_space=pltpu.VMEM)
    dma = pltpu.SemaphoreType.DMA

    def buf(*shape):
        return pltpu.VMEM(shape, BF16)

    tp_sems = [dma((n_dp, n_tp))] * 8
    results = pl.pallas_call(
        functools.partial(general_kernel, n_dp, n_ctx, n_tp, cap),
        out_shape=[
            buf(*a.shape) for a in (tokens, tokens, up_weight, down_weight)
        ],
        in_specs=[vmem, vmem, any_, any_, any_, any_],
        out_specs=[vmem] * 4,
        scratch_shapes=[
            buf(rows, feats), buf(rows, feats), buf(feats, hid), buf(hid, feats),
            buf(n_ctx, cap, feats), buf(n_ctx, cap, feats),
            buf(blocks, cap, feats), buf(blocks, cap, feats),
            buf(total, feats), buf(total, feats),
            buf(n_dp, n_tp, piece, hid), buf(n_dp, n_tp, piece, hid),
            buf(n_dp, n_tp, piece, hid), buf(n_dp, n_tp, piece, hid),
            buf(n_dp, n_tp, piece, hid), buf(n_dp, n_tp, piece, hid),
            buf(total, hid), buf(total, hid),
            buf(blocks, cap, feats), buf(blocks, cap, feats),
            buf(blocks, cap, feats), buf(blocks, cap, feats),
            dma((4,)),
            dma((blocks,)), dma((blocks,)), dma((blocks,)), dma((blocks,)),
            *tp_sems,
            dma((blocks,)), dma((blocks,)), dma((blocks,)), dma((blocks,)),
        ],
        compiler_params=pltpu.CompilerParams(
            collective_id=1, has_side_effects=True, vmem_limit_bytes=58 * 2**20
        ),
        name="general_expert_layer",
    )(expert_ids.T, gate_codes.T, tokens, cotangent, up_weight, down_weight)
    return tuple(
        pl.pallas_call(
            general_store,
            out_shape=[
                jax.ShapeDtypeStruct(a.shape, BF16)
                for a in (tokens, tokens, up_weight, down_weight)
            ],
            in_specs=[vmem] * 4,
            out_specs=[any_] * 4,
            scratch_shapes=[dma((4,))],
            compiler_params=pltpu.CompilerParams(vmem_limit_bytes=2**20),
            name="general_store",
        )(*[pltpu.with_memory_space_constraint(a, pltpu.VMEM) for a in results])
    )


def body(n_dp, n_ctx, n_tp, tokens, expert_ids, gate_codes, up_weight, down_weight, cotangent):
    rows, feats = tokens.shape
    hid = up_weight.shape[2]
    cap = rows // 16
    blocks = n_dp * n_ctx
    total = blocks * cap
    width = hid // n_tp
    near, units = units_of(n_dp, n_ctx)
    picks = expert_ids.shape[1]
    if width % 128 or n_tp != 4 or len(spans_of(units)) != 3 or near != CORES:
        return general_body(
            n_dp, n_ctx, n_tp, tokens, expert_ids, gate_codes, up_weight, down_weight, cotangent
        )
    any_ = pl.BlockSpec(memory_space=pl.ANY)
    vmem = pl.BlockSpec(memory_space=pltpu.VMEM)
    dma = pltpu.SemaphoreType.DMA

    def buf(*shape):
        return pltpu.VMEM(shape, BF16)

    block_sems = [dma((blocks,))] * 4
    tp_sems = [dma((len(units), n_tp))] * 8
    results = pl.pallas_call(
        functools.partial(kernel, n_dp, n_ctx, n_tp, cap, *plan_of(units)),
        out_shape=[
            buf(rows, feats), buf(blocks, cap, feats), buf(rows, total),
            buf(*up_weight.shape), buf(*down_weight.shape),
        ],
        in_specs=[any_] * 6,
        out_specs=[vmem] * 5,
        scratch_shapes=[
            pltpu.VMEM((picks, rows), jnp.int32), pltpu.VMEM((picks, rows), jnp.int32),
            buf(rows, feats), buf(rows, feats), buf(feats, hid), buf(hid, feats),
            buf(n_ctx, cap, feats), buf(n_ctx, cap, feats),
            buf(blocks, cap, feats), buf(blocks, cap, feats),
            buf(total, feats), buf(total, feats),
            *[buf(n_tp, total, width)] * 6,
            buf(blocks, cap, feats), buf(blocks, cap, feats), buf(blocks, cap, feats),
            buf(rows, 2 * total), buf(hid, feats), buf(feats, hid),
            dma((6,)),
            *block_sems,
            *tp_sems,
            *block_sems,
        ],
        compiler_params=pltpu.CompilerParams(
            collective_id=0, has_side_effects=True, vmem_limit_bytes=58 * 2**20
        ),
        name="expert_layer",
    )(expert_ids.T, gate_codes.T, tokens, cotangent, up_weight, down_weight)
    return tuple(
        pl.pallas_call(
            functools.partial(store, blocks),
            out_shape=[
                jax.ShapeDtypeStruct(a.shape, BF16)
                for a in (tokens, tokens, up_weight, down_weight)
            ],
            in_specs=[vmem] * 5,
            out_specs=[any_] * 4,
            scratch_shapes=[buf(rows, feats), dma((6,))],
            compiler_params=pltpu.CompilerParams(vmem_limit_bytes=8 * 2**20),
            name="store",
        )(*[pltpu.with_memory_space_constraint(a, pltpu.VMEM) for a in results])
    )


def solution(mesh):
    sizes = [mesh.shape[name] for name in ("dp", "ctx", "tp")]
    return jax.shard_map(
        functools.partial(body, *sizes),
        mesh=mesh,
        in_specs=(
            P(("dp", "ctx"), "tp"),
            P(("dp", "ctx"), None),
            P(("dp", "ctx"), None),
            P("ctx", "tp", "dp"),
            P("ctx", "dp", "tp"),
            P(("dp", "ctx"), "tp"),
        ),
        out_specs=(
            P(("dp", "ctx"), "tp"),
            P(("dp", "ctx"), "tp"),
            P("ctx", "tp", "dp"),
            P("ctx", "dp", "tp"),
        ),
        check_vma=False,
    )
```

```python
import functools

import jax
import jax.numpy as jnp
from jax import lax
from jax.experimental import pallas as pl
from jax.experimental.pallas import tpu as pltpu
from jax.sharding import PartitionSpec as P

MESH = pl.DeviceIdType.MESH
F32 = jnp.float32
BF16 = jnp.bfloat16
FIRST = (((0,), (0,)), ((), ()))
LAST = (((1,), (1,)), ((), ()))
PLAIN = (((1,), (0,)), ((), ()))
CORES = 2


def dot(a, b, how=PLAIN):
    return lax.dot_general(a, b, how, preferred_element_type=F32)


def units_of(n_dp, n_ctx):
    near = CORES if n_ctx % CORES == 0 else 1
    pairs = [(k, m) for k in range(n_dp) for m in range(n_ctx // near)]
    pairs.sort(key=lambda s: (s[0] > 0) + (s[1] > 0))
    return near, pairs


def kernel(
    n_dp, n_ctx, n_tp, cap, spans, send_order, plan,
    ids_hbm, codes_hbm, tok_hbm, cot_hbm, up_hbm, down_hbm,
    mixed, q_recv, pick_t, gup, gdown,
    ids_ref, codes_ref, tok, cot, up, down, x_send, g_send, x_recv, g_recv, x_all, g_all,
    h_send, a_send, h_recv, a_recv, act, ghid, p_send, q_send, p_recv, gate_t, up_t, down_t,
    in_sem, xs, xr, gs, gr, hs, hr, as_, ar, cs, cr, ds, dr, ps, pr, qs, qr,
):
    near, units = units_of(n_dp, n_ctx)
    d, c, t = lax.axis_index("dp"), lax.axis_index("ctx"), lax.axis_index("tp")
    n_blocks, n_chips = n_dp * n_ctx, n_ctx // near
    me = d * n_ctx + c
    chip, core = c // near, lax.rem(c, near)
    slots = n_ctx * cap
    wide = near * cap
    width = h_send.shape[2]

    loads = [
        pltpu.make_async_copy(src, dst, in_sem.at[i])
        for i, (src, dst) in enumerate((
            (ids_hbm, ids_ref), (codes_hbm, codes_ref), (tok_hbm, tok),
            (cot_hbm, cot), (up_hbm.at[0], up), (down_hbm.at[0], down),
        ))
    ]

    def peer(u, i, sign):
        k, m = units[u]
        g = lax.rem(d + (k if sign > 0 else n_dp - k), n_dp)
        p = lax.rem(chip + (m if sign > 0 else n_chips - m), n_chips)
        e = p * near + lax.rem(core + (i if sign > 0 else near - i), near)
        return g, e, {"dp": g, "ctx": e}

    others = [(u, i) for u in range(len(units)) for i in range(near) if u or i]

    def tp_dev(m):
        j = (t + 1 - 2 * lax.rem(t, 2), lax.rem(t + 2, 4), 3 - t)[m - 1]
        return j, {"tp": j}

    barrier = pltpu.get_barrier_semaphore()
    for u, i in others:
        pl.semaphore_signal(barrier, inc=1, device_id=peer(u, i, 1)[2], device_id_type=MESH)
    for m in range(1, n_tp):
        pl.semaphore_signal(barrier, inc=1, device_id=tp_dev(m)[1], device_id_type=MESH)
    for load in loads[:3]:
        load.start()
    for load in loads[3:]:
        load.start()

    picks, rows = ids_ref.shape
    lane = lax.broadcasted_iota(jnp.int32, (slots, rows), 0)
    lane_e = jnp.zeros((slots, rows), jnp.int32)
    for e in range(1, n_ctx):
        lane_e = lane_e + (lane >= e * cap).astype(jnp.int32)
    lane_s = lane - lane_e * cap
    earlier = (
        lax.broadcasted_iota(jnp.int32, (rows, rows), 0)
        < lax.broadcasted_iota(jnp.int32, (rows, rows), 1)
    ).astype(F32).astype(BF16)
    named = jnp.zeros((slots, rows), jnp.int32)
    code = jnp.zeros((slots, rows), jnp.int32)
    loads[0].wait()
    loads[1].wait()
    ids, codes = ids_ref[...], codes_ref[...]
    for k in range(picks):
        hit = ids[k : k + 1] == lane_e
        named = jnp.where(hit, 1, named)
        code = jnp.where(hit, codes[k : k + 1], code)
    rank = dot(named.astype(F32).astype(BF16), earlier)
    chosen = jnp.where(rank == lane_s.astype(F32), named, 0)
    code = chosen * code
    pick = chosen.astype(F32).astype(BF16)
    gate = jnp.sum(code.astype(F32), axis=1, keepdims=True) * (1.0 / 32768.0)

    def remote(src, dst, send, recv, dev):
        return pltpu.make_async_remote_copy(
            src, dst, send, recv, device_id=dev, device_id_type=MESH
        )

    def put_blocks(ref, first, value, count):
        for b in range(count):
            ref[first + b] = value[b * cap : (b + 1) * cap].astype(BF16)

    def join(parts):
        return jnp.concatenate([p.astype(F32) for p in parts], axis=0).astype(BF16)

    def span_of(u):
        return [u in range(first, first + count) for first, count in spans].index(True)

    def taken(part, sem):
        remote(part, part, sem, sem, tp_dev(1)[1]).wait_recv()

    def scatter_rows(order, send, recv, send_sem, recv_sem):
        for u in order:
            for i in range(near):
                pos = u * near + i
                if pos:
                    _, e, dev = peer(u, i, 1)
                    remote(
                        send.at[e], recv.at[pos], send_sem.at[0], recv_sem.at[span_of(u)], dev
                    ).start()

    def at(u):
        first, count = spans[u]
        return slice(first * wide, (first + count) * wide)

    def ds_of(u):
        first, count = spans[u]
        return pl.ds(first * wide, count * wide)

    def members(u):
        first, count = spans[u]
        return [(v, i, v * near + i) for v in range(first, first + count) for i in range(near)]

    def collect(u, send, recv, recv_sem, into):
        held = [pos for v, i, pos in members(u)]
        first = max(1, held[0])
        taken(recv.at[pl.ds(first, held[-1] + 1 - first)], recv_sem.at[u])
        parts = [recv[pos] if pos else send[c] for pos in held]
        value = join(parts)
        into[at(u)] = value
        return value

    def cut(u, value, send):
        for j in range(n_tp):
            send[j, at(u)] = value[:, j * width : (j + 1) * width].astype(send.dtype)

    def tp_scatter(u, send, recv, send_sem, recv_sem):
        for m in range(1, n_tp):
            j, dev = tp_dev(m)
            remote(
                send.at[j, ds_of(u)], recv.at[m, ds_of(u)],
                send_sem.at[0], recv_sem.at[u], dev,
            ).start()

    def tp_total(u, send, recv, recv_sem):
        value = send[t, at(u)].astype(F32)
        taken(recv.at[pl.ds(1, n_tp - 1), ds_of(u)], recv_sem.at[u])
        for m in range(1, n_tp):
            value = value + recv[m, at(u)].astype(F32)
        return value

    def tp_gather(u, buf, send_sem, recv_sem):
        part = buf.at[t, ds_of(u)]
        for m in range(1, n_tp):
            remote(part, part, send_sem.at[0], recv_sem.at[u], tp_dev(m)[1]).start()

    def whole(u, buf, recv_sem):
        taken(buf.at[pl.ds(0, n_tp - 1), ds_of(u)], recv_sem.at[u])
        return jnp.concatenate([buf[j, at(u)] for j in range(n_tp)], axis=1)

    def give_back(u, value, send, recv, send_sem, recv_sem):
        put_blocks(send, spans[u][0] * near, value, spans[u][1] * near)
        for v, i, pos in sorted(members(u), key=lambda w: -w[0]):
            if pos:
                remote(
                    send.at[pos], recv.at[me], send_sem.at[0], recv_sem.at[0],
                    peer(v, i, -1)[2],
                ).start()
            else:
                recv[me] = send[0]

    def returned(recv, recv_sem):
        taken(recv.at[pl.ds(0, len(others))], recv_sem.at[0])

    def left(part, sem):
        remote(part, part, sem.at[0], sem.at[0], tp_dev(1)[1]).wait_send()

    loads[2].wait()
    put_blocks(x_send, 0, dot(pick, tok[...]), n_ctx)
    pl.semaphore_wait(barrier, len(others) + n_tp - 1)
    early = [kind for kind, u in send_order].index("g")
    scatter_rows([u for kind, u in send_order[:early]], x_send, x_recv, xs, xr)
    loads[3].wait()
    put_blocks(g_send, 0, dot(pick, cot[...]) * gate, n_ctx)
    for kind, u in send_order[early:]:
        if kind == "x":
            scatter_rows([u], x_send, x_recv, xs, xr)
        else:
            scatter_rows([u], g_send, g_recv, gs, gr)

    def start_hidden(u):
        value = dot(collect(u, x_send, x_recv, xr, x_all), up[...])
        cut(u, value, h_send)
        tp_scatter(u, h_send, h_recv, hs, hr)

    def start_grad(u):
        g = collect(u, g_send, g_recv, gr, g_all)
        value = dot(g, down_t[...]) if u else dot(g, down[...], LAST)
        cut(u, value, a_send)
        tp_scatter(u, a_send, a_recv, as_, ar)

    slopes = {}

    def activate(u):
        hidden = tp_total(u, h_send, h_recv, hr)
        sigma = 1.0 / (1.0 + jnp.exp(-hidden))
        act[t, at(u)] = (hidden * sigma).astype(BF16)
        slopes[u] = sigma * (1.0 + hidden * (1.0 - sigma))

    def give_act(u):
        tp_gather(u, act, cs, cr)

    def grade(u):
        ghid[t, at(u)] = (tp_total(u, a_send, a_recv, ar) * slopes[u]).astype(BF16)

    def give_ghid(u):
        tp_gather(u, ghid, ds, dr)

    def produce(u):
        value = dot(whole(u, act, cr), down[...])
        give_back(u, value, p_send, p_recv, ps, pr)

    def to_inputs(u):
        value = dot(whole(u, ghid, dr), up_t[...])
        give_back(u, value, q_send, q_recv, qs, qr)

    def turn(u):
        high = lax.shift_right_logical(code, 8)
        gate_hi = (high.astype(F32) * (1.0 / 128.0)).astype(BF16)
        gate_lo = ((code - high * 256).astype(F32) * (1.0 / 32768.0)).astype(BF16)
        twice = jnp.concatenate([pick.astype(F32)] * n_dp, axis=0)
        pick_t[...] = twice.T.astype(BF16)
        gates = jnp.concatenate(
            [gate_hi.astype(F32)] * n_dp + [gate_lo.astype(F32)] * n_dp, axis=0
        )
        gate_t[...] = gates.T.astype(BF16)
        up_t[...] = up[...].T
        down_t[...] = down[...].T

    def columns(buf):
        return jnp.concatenate([buf[j] for j in range(n_tp)], axis=1)

    def grad_down(u):
        gdown[0] = dot(columns(act), g_all[...], FIRST).astype(BF16)

    def grad_up(u):
        gup[0] = dot(x_all[...], columns(ghid), FIRST).astype(BF16)

    def mix(u):
        returned(p_recv, pr)
        got = join([p_recv[b] for b in range(n_blocks)])
        half = n_blocks * cap
        mixed[...] = (dot(gate_t[:, :half], got) + dot(gate_t[:, half:], got)).astype(BF16)

    def wait_up(u):
        loads[4].wait()

    def wait_down(u):
        loads[5].wait()

    def sent(u):
        for buf, sem in ((x_recv, xs), (g_recv, gs), (p_send, ps)):
            left(buf.at[pl.ds(0, len(others))], sem)
        for buf, sem in ((h_send, hs), (a_send, as_), (act, cs), (ghid, ds)):
            left(buf.at[pl.ds(0, n_tp - 1)], sem)

    steps = {
        "sent": sent,
        "up": wait_up, "down": wait_down, "h": start_hidden, "a": start_grad, "turn": turn,
        "act": activate, "ghid": grade, "p": produce, "q": to_inputs,
        "ga": give_act, "gg": give_ghid,
        "gdown": grad_down, "gup": grad_up, "mix": mix,
    }
    for name, u in plan:
        steps[name](u)
    returned(q_recv, qr)

    left(q_send.at[pl.ds(0, len(others))], qs)


STEPS = (
    "up", "h0", "down", "a0", "turn", "h1", "a1", "act0", "ghid0", "h2",
    "act1", "ga1", "a2", "act2", "ga2", "ghid1", "gg1", "p1", "ghid2", "gg2",
    "ga0", "gg0", "p2", "q1", "q2", "p0", "q0", "sent", "gdown", "gup",
    "mix",
)
SENDS = (
    "x1", "x0", "g1", "g0", "x2", "g2",
)


def spans_of(units):
    hops = [(k > 0) + (m > 0) for k, m in units]
    return [(hops.index(h), hops.count(h)) for h in sorted(set(hops))]


def pairs_of(words):
    pairs = []
    for word in words:
        name = word.rstrip("0123456789")
        pairs.append((name, int(word[len(name) :] or 0)))
    return pairs


def plan_of(units):
    spans = spans_of(units)
    sends = [
        (name, u) for name, w in pairs_of(SENDS) for u in range(spans[w][0], sum(spans[w]))[::-1]
    ]
    return spans, sends, pairs_of(STEPS)


def store(n_blocks, mixed, q_recv, pick_t, gup, gdown, mixed_o, gtok_o, gup_o, gdown_o, gtok, sem):
    copies = [
        pltpu.make_async_copy(src, dst, sem.at[i])
        for i, (src, dst) in enumerate(((gup, gup_o), (gdown, gdown_o), (mixed, mixed_o)))
    ]
    for copy in copies:
        copy.start()
    got = jnp.concatenate([q_recv[b].astype(F32) for b in range(n_blocks)], axis=0).astype(BF16)
    rows = gtok.shape[0]
    parts = 3 if rows % 48 == 0 else 1
    step = rows // parts
    for i in range(parts):
        here = slice(i * step, (i + 1) * step)
        gtok[here] = dot(pick_t[here], got).astype(BF16)
        part = pl.ds(i * step, step)
        copy = pltpu.make_async_copy(gtok.at[part], gtok_o.at[part], sem.at[3 + i])
        copy.start()
        copies.append(copy)
    for copy in copies:
        copy.wait()


def general_kernel(
    n_dp, n_ctx, n_tp, cap,
    ids_ref, codes_ref, tok_hbm, cot_hbm, up_hbm, down_hbm,
    mixed, gtok, gup, gdown,
    tok, cot, up, down, x_send, g_send, x_recv, g_recv, x_all, g_all,
    h_send, a_send, h_recv, a_recv, act, ghid, act_all, ghid_all,
    p_send, q_send, p_recv, q_recv,
    in_sem, xs, xr, gs, gr, hs, hr, as_, ar, cs, cr, ds, dr, ps, pr, qs, qr,
):
    d, c, t = lax.axis_index("dp"), lax.axis_index("ctx"), lax.axis_index("tp")
    n_blocks = n_dp * n_ctx
    me = d * n_ctx + c
    slots = n_ctx * cap

    loads = [
        pltpu.make_async_copy(src, dst, in_sem.at[i])
        for i, (src, dst) in enumerate(
            ((tok_hbm, tok), (cot_hbm, cot), (up_hbm.at[0], up), (down_hbm.at[0], down))
        )
    ]
    for load in loads:
        load.start()

    def block_dev(k):
        b = lax.rem(me + k, n_blocks)
        return b, {"dp": b // n_ctx, "ctx": lax.rem(b, n_ctx)}

    def tp_dev(k):
        j = lax.rem(t + k, n_tp)
        return j, {"tp": j}

    barrier = pltpu.get_barrier_semaphore()
    for k in range(1, n_blocks):
        pl.semaphore_signal(barrier, inc=1, device_id=block_dev(k)[1], device_id_type=MESH)
    for k in range(1, n_tp):
        pl.semaphore_signal(barrier, inc=1, device_id=tp_dev(k)[1], device_id_type=MESH)

    picks, rows = ids_ref.shape
    lane = lax.broadcasted_iota(jnp.int32, (slots, rows), 0)
    lane_e = jnp.zeros((slots, rows), jnp.int32)
    for e in range(1, n_ctx):
        lane_e = lane_e + (lane >= e * cap).astype(jnp.int32)
    lane_s = lane - lane_e * cap
    named = jnp.zeros((slots, rows), jnp.int32)
    code = jnp.zeros((slots, rows), jnp.int32)
    ids, codes = ids_ref[...], codes_ref[...]
    for k in range(picks):
        hit = ids[k : k + 1] == lane_e
        named = jnp.where(hit, 1, named)
        code = jnp.where(hit, codes[k : k + 1], code)
    earlier = (
        lax.broadcasted_iota(jnp.int32, (rows, rows), 0)
        < lax.broadcasted_iota(jnp.int32, (rows, rows), 1)
    )
    rank = dot(named.astype(F32).astype(BF16), earlier.astype(F32).astype(BF16))
    chosen = jnp.where(rank == lane_s.astype(F32), named, 0)
    code = chosen * code
    pick = chosen.astype(F32).astype(BF16)
    high = lax.shift_right_logical(code, 8)
    gate_hi = (high.astype(F32) * (1.0 / 128.0)).astype(BF16)
    gate_lo = ((code - high * 256).astype(F32) * (1.0 / 32768.0)).astype(BF16)

    def groups_dev(g, cc):
        return {"dp": g, "ctx": cc}

    def others(k):
        return range(1 if k == 0 else 0, n_ctx)

    def to(k, m):
        return lax.rem(d + k, n_dp), lax.rem(c + m, n_ctx)

    def spread(send, recv, send_sem, recv_sem, k, back=False):
        for m in others(k):
            g, e = to(k, m)
            src = send.at[g * n_ctx + e] if back else send.at[e]
            pltpu.make_async_remote_copy(
                src, recv.at[me], send_sem.at[k * n_ctx + m], recv_sem.at[me],
                device_id=groups_dev(g, e), device_id_type=MESH,
            ).start()
        if k == 0:
            recv[me] = send[me] if back else send[c]

    def arrived(recv, recv_sem, k):
        g = lax.rem(d + n_dp - k, n_dp)
        for m in others(k):
            e = lax.rem(c + m, n_ctx)
            b = g * n_ctx + e
            pltpu.make_async_remote_copy(
                recv.at[b], recv.at[b], recv_sem.at[b], recv_sem.at[b],
                device_id=groups_dev(g, e), device_id_type=MESH,
            ).wait_recv()
        return g

    def sent(send, send_sem):
        for k in range(n_dp):
            for m in others(k):
                g, e = to(k, m)
                i = k * n_ctx + m
                pltpu.make_async_remote_copy(
                    send.at[0], send.at[0], send_sem.at[i], send_sem.at[i],
                    device_id=groups_dev(g, e), device_id_type=MESH,
                ).wait_send()

    def put_blocks(ref, first, value, count):
        for b in range(count):
            ref[first + b] = value[b * cap : (b + 1) * cap].astype(BF16)

    def take_blocks(ref, first, count):
        return jnp.concatenate(
            [ref[first + b].astype(F32) for b in range(count)], axis=0
        ).astype(BF16)

    def tp_scatter(send, recv, send_sem, recv_sem, k):
        for m in range(1, n_tp):
            j, dev = tp_dev(m)
            pltpu.make_async_remote_copy(
                send.at[k, j], recv.at[k, t], send_sem.at[k, m], recv_sem.at[k, t],
                device_id=dev, device_id_type=MESH,
            ).start()

    def tp_gather(buf, send_sem, recv_sem, k):
        for m in range(1, n_tp):
            j, dev = tp_dev(m)
            pltpu.make_async_remote_copy(
                buf.at[k, t], buf.at[k, t], send_sem.at[k, m], recv_sem.at[k, t],
                device_id=dev, device_id_type=MESH,
            ).start()

    def tp_arrived(buf, recv_sem, k):
        for m in range(1, n_tp):
            j, dev = tp_dev(m)
            pltpu.make_async_remote_copy(
                buf.at[k, j], buf.at[k, j], recv_sem.at[k, j], recv_sem.at[k, j],
                device_id=dev, device_id_type=MESH,
            ).wait_recv()

    def tp_sent(buf, send_sem):
        for k in range(n_dp):
            for m in range(1, n_tp):
                j, dev = tp_dev(m)
                pltpu.make_async_remote_copy(
                    buf.at[k, 0], buf.at[k, 0], send_sem.at[k, m], send_sem.at[k, m],
                    device_id=dev, device_id_type=MESH,
                ).wait_send()

    forth, back = list(range(n_dp)), list(reversed(range(n_dp)))
    loads[0].wait()
    put_blocks(x_send, 0, dot(pick, tok[...]), n_ctx)
    pl.semaphore_wait(barrier, n_blocks - 1 + n_tp - 1)
    for k in forth:
        spread(x_send, x_recv, xs, xr, k)
    loads[1].wait()
    put_blocks(g_send, 0, dot(gate_hi, cot[...]) + dot(gate_lo, cot[...]), n_ctx)
    for k in back:
        spread(g_send, g_recv, gs, gr, k)

    group = slots
    piece = group // n_tp

    def put_pieces(ref, k, value):
        for j in range(n_tp):
            ref[k, j] = value[j * piece : (j + 1) * piece].astype(BF16)

    def total(send, recv, k):
        value = send[k, t].astype(F32)
        for m in range(1, n_tp):
            value = value + recv[k, lax.rem(t + m, n_tp)].astype(F32)
        return value

    loads[2].wait()
    for k in forth:
        g = arrived(x_recv, xr, k)
        x_all[k * group : (k + 1) * group] = take_blocks(x_recv, g * n_ctx, n_ctx)
        put_pieces(h_send, k, dot(x_all[k * group : (k + 1) * group], up[...]))
        tp_scatter(h_send, h_recv, hs, hr, k)
    slopes = [None] * n_dp
    for k in forth:
        tp_arrived(h_recv, hr, k)
        hidden = total(h_send, h_recv, k)
        sigma = 1.0 / (1.0 + jnp.exp(-hidden))
        act[k, t] = (hidden * sigma).astype(BF16)
        tp_gather(act, cs, cr, k)
        slopes[k] = sigma * (1.0 + hidden * (1.0 - sigma))
    loads[3].wait()
    for k in back:
        g = arrived(g_recv, gr, k)
        g_all[k * group : (k + 1) * group] = take_blocks(g_recv, g * n_ctx, n_ctx)
        put_pieces(a_send, k, dot(g_all[k * group : (k + 1) * group], down[...], LAST))
        tp_scatter(a_send, a_recv, as_, ar, k)

    def whole(buf, k):
        return jnp.concatenate([buf[k, j].astype(F32) for j in range(n_tp)], axis=0).astype(BF16)

    def home(k):
        return lax.rem(d + n_dp - k, n_dp) * n_ctx, (n_dp - k) % n_dp

    for k in back:
        rows_k = slice(k * group, (k + 1) * group)
        first, to_k = home(k)
        tp_arrived(act, cr, k)
        act_all[rows_k] = whole(act, k)
        put_blocks(p_send, first, dot(act_all[rows_k], down[...]), n_ctx)
        spread(p_send, p_recv, ps, pr, to_k, back=True)
    for k in back:
        tp_arrived(a_recv, ar, k)
        ghid[k, t] = (total(a_send, a_recv, k) * slopes[k]).astype(BF16)
        tp_gather(ghid, ds, dr, k)
    for k in back:
        rows_k = slice(k * group, (k + 1) * group)
        first, to_k = home(k)
        tp_arrived(ghid, dr, k)
        ghid_all[rows_k] = whole(ghid, k)
        put_blocks(q_send, first, dot(ghid_all[rows_k], up[...], LAST), n_ctx)
        spread(q_send, q_recv, qs, qr, to_k, back=True)

    gdown[0] = dot(act_all[...], g_all[...], FIRST).astype(BF16)
    gup[0] = dot(x_all[...], ghid_all[...], FIRST).astype(BF16)

    for k in back:
        arrived(p_recv, pr, k)
    out = jnp.zeros(mixed.shape, F32)
    for g in range(n_dp):
        got = take_blocks(p_recv, g * n_ctx, n_ctx)
        out = out + dot(gate_hi, got, FIRST) + dot(gate_lo, got, FIRST)
    mixed[...] = out.astype(BF16)
    for k in back:
        arrived(q_recv, qr, k)
    out = jnp.zeros(gtok.shape, F32)
    for g in range(n_dp):
        out = out + dot(pick, take_blocks(q_recv, g * n_ctx, n_ctx), FIRST)
    gtok[...] = out.astype(BF16)

    sent(x_send, xs)
    sent(g_send, gs)
    tp_sent(h_recv, hs)
    tp_sent(a_recv, as_)
    tp_sent(act, cs)
    tp_sent(ghid, ds)
    sent(p_send, ps)
    sent(q_send, qs)


def general_store(*refs):
    sem = refs[-1]
    copies = [
        pltpu.make_async_copy(src, dst, sem.at[i])
        for i, (src, dst) in enumerate(zip(refs[:4], refs[4:8]))
    ]
    for copy in copies:
        copy.start()
    for copy in copies:
        copy.wait()


def general_body(n_dp, n_ctx, n_tp, tokens, expert_ids, gate_codes, up_weight, down_weight, cotangent):
    rows, feats = tokens.shape
    hid = up_weight.shape[2]
    cap = rows // 16
    blocks = n_dp * n_ctx
    total = blocks * cap
    piece = n_ctx * cap // n_tp
    any_ = pl.BlockSpec(memory_space=pl.ANY)
    vmem = pl.BlockSpec(memory_space=pltpu.VMEM)
    dma = pltpu.SemaphoreType.DMA

    def buf(*shape):
        return pltpu.VMEM(shape, BF16)

    tp_sems = [dma((n_dp, n_tp))] * 8
    results = pl.pallas_call(
        functools.partial(general_kernel, n_dp, n_ctx, n_tp, cap),
        out_shape=[
            buf(*a.shape) for a in (tokens, tokens, up_weight, down_weight)
        ],
        in_specs=[vmem, vmem, any_, any_, any_, any_],
        out_specs=[vmem] * 4,
        scratch_shapes=[
            buf(rows, feats), buf(rows, feats), buf(feats, hid), buf(hid, feats),
            buf(n_ctx, cap, feats), buf(n_ctx, cap, feats),
            buf(blocks, cap, feats), buf(blocks, cap, feats),
            buf(total, feats), buf(total, feats),
            buf(n_dp, n_tp, piece, hid), buf(n_dp, n_tp, piece, hid),
            buf(n_dp, n_tp, piece, hid), buf(n_dp, n_tp, piece, hid),
            buf(n_dp, n_tp, piece, hid), buf(n_dp, n_tp, piece, hid),
            buf(total, hid), buf(total, hid),
            buf(blocks, cap, feats), buf(blocks, cap, feats),
            buf(blocks, cap, feats), buf(blocks, cap, feats),
            dma((4,)),
            dma((blocks,)), dma((blocks,)), dma((blocks,)), dma((blocks,)),
            *tp_sems,
            dma((blocks,)), dma((blocks,)), dma((blocks,)), dma((blocks,)),
        ],
        compiler_params=pltpu.CompilerParams(
            collective_id=1, has_side_effects=True, vmem_limit_bytes=58 * 2**20
        ),
        name="general_expert_layer",
    )(expert_ids.T, gate_codes.T, tokens, cotangent, up_weight, down_weight)
    return tuple(
        pl.pallas_call(
            general_store,
            out_shape=[
                jax.ShapeDtypeStruct(a.shape, BF16)
                for a in (tokens, tokens, up_weight, down_weight)
            ],
            in_specs=[vmem] * 4,
            out_specs=[any_] * 4,
            scratch_shapes=[dma((4,))],
            compiler_params=pltpu.CompilerParams(vmem_limit_bytes=2**20),
            name="general_store",
        )(*[pltpu.with_memory_space_constraint(a, pltpu.VMEM) for a in results])
    )


def body(n_dp, n_ctx, n_tp, tokens, expert_ids, gate_codes, up_weight, down_weight, cotangent):
    rows, feats = tokens.shape
    hid = up_weight.shape[2]
    cap = rows // 16
    blocks = n_dp * n_ctx
    total = blocks * cap
    width = hid // n_tp
    near, units = units_of(n_dp, n_ctx)
    picks = expert_ids.shape[1]
    if width % 128 or n_tp != 4 or len(spans_of(units)) != 3 or near != CORES:
        return general_body(
            n_dp, n_ctx, n_tp, tokens, expert_ids, gate_codes, up_weight, down_weight, cotangent
        )
    any_ = pl.BlockSpec(memory_space=pl.ANY)
    vmem = pl.BlockSpec(memory_space=pltpu.VMEM)
    dma = pltpu.SemaphoreType.DMA

    def buf(*shape):
        return pltpu.VMEM(shape, BF16)

    shared, spanned = dma((1,)), dma((len(spans_of(units)),))
    results = pl.pallas_call(
        functools.partial(kernel, n_dp, n_ctx, n_tp, cap, *plan_of(units)),
        out_shape=[
            buf(rows, feats), buf(blocks, cap, feats), buf(rows, total),
            buf(*up_weight.shape), buf(*down_weight.shape),
        ],
        in_specs=[any_] * 6,
        out_specs=[vmem] * 5,
        scratch_shapes=[
            pltpu.VMEM((picks, rows), jnp.int32), pltpu.VMEM((picks, rows), jnp.int32),
            buf(rows, feats), buf(rows, feats), buf(feats, hid), buf(hid, feats),
            buf(n_ctx, cap, feats), buf(n_ctx, cap, feats),
            buf(blocks, cap, feats), buf(blocks, cap, feats),
            buf(total, feats), buf(total, feats),
            *[buf(n_tp, total, width)] * 6,
            buf(blocks, cap, feats), buf(blocks, cap, feats), buf(blocks, cap, feats),
            buf(rows, 2 * total), buf(hid, feats), buf(feats, hid),
            dma((6,)),
            *[shared, spanned] * 6,
            *[shared] * 4,
        ],
        compiler_params=pltpu.CompilerParams(
            collective_id=0, has_side_effects=True, vmem_limit_bytes=58 * 2**20
        ),
        name="expert_layer",
    )(expert_ids.T, gate_codes.T, tokens, cotangent, up_weight, down_weight)
    return tuple(
        pl.pallas_call(
            functools.partial(store, blocks),
            out_shape=[
                jax.ShapeDtypeStruct(a.shape, BF16)
                for a in (tokens, tokens, up_weight, down_weight)
            ],
            in_specs=[vmem] * 5,
            out_specs=[any_] * 4,
            scratch_shapes=[buf(rows, feats), dma((6,))],
            compiler_params=pltpu.CompilerParams(vmem_limit_bytes=8 * 2**20),
            name="store",
        )(*[pltpu.with_memory_space_constraint(a, pltpu.VMEM) for a in results])
    )


def solution(mesh):
    sizes = [mesh.shape[name] for name in ("dp", "ctx", "tp")]
    return jax.shard_map(
        functools.partial(body, *sizes),
        mesh=mesh,
        in_specs=(
            P(("dp", "ctx"), "tp"),
            P(("dp", "ctx"), None),
            P(("dp", "ctx"), None),
            P("ctx", "tp", "dp"),
            P("ctx", "dp", "tp"),
            P(("dp", "ctx"), "tp"),
        ),
        out_specs=(
            P(("dp", "ctx"), "tp"),
            P(("dp", "ctx"), "tp"),
            P("ctx", "tp", "dp"),
            P("ctx", "dp", "tp"),
        ),
        check_vma=False,
    )
```

```python
import functools

import jax
import jax.numpy as jnp
from jax import lax
from jax.experimental import pallas as pl
from jax.experimental.pallas import tpu as pltpu
from jax.sharding import PartitionSpec as P

MESH = pl.DeviceIdType.MESH
F32 = jnp.float32
BF16 = jnp.bfloat16
FIRST = (((0,), (0,)), ((), ()))
LAST = (((1,), (1,)), ((), ()))
PLAIN = (((1,), (0,)), ((), ()))
CORES = 2


def dot(a, b, how=PLAIN):
    return lax.dot_general(a, b, how, preferred_element_type=F32)


def units_of(n_dp, n_ctx):
    near = CORES if n_ctx % CORES == 0 else 1
    pairs = [(k, m) for k in range(n_dp) for m in range(n_ctx // near)]
    pairs.sort(key=lambda s: (s[0] > 0) + (s[1] > 0))
    return near, pairs


def kernel(
    n_dp, n_ctx, n_tp, cap, spans, send_order, plan,
    ids_hbm, codes_hbm, tok_hbm, cot_hbm, up_hbm, down_hbm,
    mixed, q_recv, pick_t, gup, gdown,
    picked, tok, cot, up, down, x_send, g_send, x_recv, g_recv, x_all, g_all,
    h_send, a_send, h_recv, a_recv, act, ghid, p_send, q_send, p_recv, gate_t, up_t, down_t,
    in_sem, xs, xr, gs, gr, hs, hr, as_, ar, cs, cr, ds, dr, ps, pr, qs, qr,
):
    near, units = units_of(n_dp, n_ctx)
    d, c, t = lax.axis_index("dp"), lax.axis_index("ctx"), lax.axis_index("tp")
    n_blocks, n_chips = n_dp * n_ctx, n_ctx // near
    me = d * n_ctx + c
    chip, core = c // near, lax.rem(c, near)
    slots = n_ctx * cap
    wide = near * cap
    width = h_send.shape[2]

    loads = [
        pltpu.make_async_copy(src, dst, in_sem.at[max(0, i - 1)])
        for i, (src, dst) in enumerate((
            (ids_hbm, picked.at[0]), (codes_hbm, picked.at[1]), (tok_hbm, tok),
            (cot_hbm, cot), (up_hbm.at[0], up), (down_hbm.at[0], down),
        ))
    ]

    def peer(u, i, sign):
        k, m = units[u]
        g = lax.rem(d + (k if sign > 0 else n_dp - k), n_dp)
        p = lax.rem(chip + (m if sign > 0 else n_chips - m), n_chips)
        e = p * near + lax.rem(core + (i if sign > 0 else near - i), near)
        return g, e, {"dp": g, "ctx": e}

    others = [(u, i) for u in range(len(units)) for i in range(near) if u or i]

    def tp_dev(m):
        j = (t + 1 - 2 * lax.rem(t, 2), lax.rem(t + 2, 4), 3 - t)[m - 1]
        return j, {"tp": j}

    barrier = pltpu.get_barrier_semaphore()
    for u, i in others:
        pl.semaphore_signal(barrier, inc=1, device_id=peer(u, i, 1)[2], device_id_type=MESH)
    for m in range(1, n_tp):
        pl.semaphore_signal(barrier, inc=1, device_id=tp_dev(m)[1], device_id_type=MESH)
    for load in loads[:3]:
        load.start()
    for load in loads[3:]:
        load.start()

    _, picks, rows = picked.shape
    lane = lax.broadcasted_iota(jnp.int32, (slots, rows), 0)
    lane_e = jnp.zeros((slots, rows), jnp.int32)
    for e in range(1, n_ctx):
        lane_e = lane_e + (lane >= e * cap).astype(jnp.int32)
    lane_s = lane - lane_e * cap
    earlier = (
        lax.broadcasted_iota(jnp.int32, (rows, rows), 0)
        < lax.broadcasted_iota(jnp.int32, (rows, rows), 1)
    ).astype(F32).astype(BF16)
    named = jnp.zeros((slots, rows), jnp.int32)
    code = jnp.zeros((slots, rows), jnp.int32)
    pltpu.make_async_copy(picked, picked, in_sem.at[0]).wait()
    ids, codes = picked[0], picked[1]
    for k in range(picks):
        hit = ids[k : k + 1] == lane_e
        named = jnp.where(hit, 1, named)
        code = jnp.where(hit, codes[k : k + 1], code)
    rank = dot(named.astype(F32).astype(BF16), earlier)
    chosen = jnp.where(rank == lane_s.astype(F32), named, 0)
    code = chosen * code
    pick = chosen.astype(F32).astype(BF16)
    gate = jnp.sum(code.astype(F32), axis=1, keepdims=True) * (1.0 / 32768.0)

    def remote(src, dst, send, recv, dev):
        return pltpu.make_async_remote_copy(
            src, dst, send, recv, device_id=dev, device_id_type=MESH
        )

    def put_blocks(ref, first, value, count):
        for b in range(count):
            ref[first + b] = value[b * cap : (b + 1) * cap].astype(BF16)

    def join(parts):
        return jnp.concatenate([p.astype(F32) for p in parts], axis=0).astype(BF16)

    def span_of(u):
        return [u in range(first, first + count) for first, count in spans].index(True)

    def taken(part, sem):
        remote(part, part, sem, sem, tp_dev(1)[1]).wait_recv()

    def scatter_rows(order, send, recv, send_sem, recv_sem):
        for u in order:
            for i in range(near):
                pos = u * near + i
                if pos:
                    _, e, dev = peer(u, i, 1)
                    remote(
                        send.at[e], recv.at[pos], send_sem.at[0], recv_sem.at[span_of(u)], dev
                    ).start()

    def at(u):
        first, count = spans[u]
        return slice(first * wide, (first + count) * wide)

    def ds_of(u):
        first, count = spans[u]
        return pl.ds(first * wide, count * wide)

    def members(u):
        first, count = spans[u]
        return [(v, i, v * near + i) for v in range(first, first + count) for i in range(near)]

    def collect(u, send, recv, recv_sem, into):
        held = [pos for v, i, pos in members(u)]
        first = max(1, held[0])
        taken(recv.at[pl.ds(first, held[-1] + 1 - first)], recv_sem.at[u])
        parts = [recv[pos] if pos else send[c] for pos in held]
        value = join(parts)
        into[at(u)] = value
        return value

    def cut(u, value, send):
        for j in range(n_tp):
            send[j, at(u)] = value[:, j * width : (j + 1) * width].astype(send.dtype)

    def tp_scatter(u, send, recv, send_sem, recv_sem):
        for m in range(1, n_tp):
            j, dev = tp_dev(m)
            remote(
                send.at[j, ds_of(u)], recv.at[m, ds_of(u)],
                send_sem.at[0], recv_sem.at[u], dev,
            ).start()

    def tp_total(u, send, recv, recv_sem):
        value = send[t, at(u)].astype(F32)
        taken(recv.at[pl.ds(1, n_tp - 1), ds_of(u)], recv_sem.at[u])
        for m in range(1, n_tp):
            value = value + recv[m, at(u)].astype(F32)
        return value

    def tp_gather(u, buf, send_sem, recv_sem):
        part = buf.at[t, ds_of(u)]
        for m in range(1, n_tp):
            remote(part, part, send_sem.at[0], recv_sem.at[u], tp_dev(m)[1]).start()

    def whole(u, buf, recv_sem):
        taken(buf.at[pl.ds(0, n_tp - 1), ds_of(u)], recv_sem.at[u])
        return jnp.concatenate([buf[j, at(u)] for j in range(n_tp)], axis=1)

    def give_back(u, value, send, recv, send_sem, recv_sem):
        put_blocks(send, spans[u][0] * near, value, spans[u][1] * near)
        for v, i, pos in sorted(members(u), key=lambda w: -w[0]):
            if pos:
                remote(
                    send.at[pos], recv.at[me], send_sem.at[0], recv_sem.at[0],
                    peer(v, i, -1)[2],
                ).start()
            else:
                recv[me] = send[0]

    def returned(recv, recv_sem):
        taken(recv.at[pl.ds(0, len(others))], recv_sem.at[0])

    def left(part, sem):
        remote(part, part, sem.at[0], sem.at[0], tp_dev(1)[1]).wait_send()

    loads[2].wait()
    put_blocks(x_send, 0, dot(pick, tok[...]), n_ctx)
    pl.semaphore_wait(barrier, len(others) + n_tp - 1)
    early = [kind for kind, u in send_order].index("g")
    scatter_rows([u for kind, u in send_order[:early]], x_send, x_recv, xs, xr)
    loads[3].wait()
    put_blocks(g_send, 0, dot(pick, cot[...]) * gate, n_ctx)
    for kind, u in send_order[early:]:
        if kind == "x":
            scatter_rows([u], x_send, x_recv, xs, xr)
        else:
            scatter_rows([u], g_send, g_recv, gs, gr)

    def start_hidden(u):
        value = dot(collect(u, x_send, x_recv, xr, x_all), up[...])
        cut(u, value, h_send)
        tp_scatter(u, h_send, h_recv, hs, hr)

    def start_grad(u):
        g = collect(u, g_send, g_recv, gr, g_all)
        value = dot(g, down_t[...]) if u else dot(g, down[...], LAST)
        cut(u, value, a_send)
        tp_scatter(u, a_send, a_recv, as_, ar)

    slopes = {}

    def activate(u):
        hidden = tp_total(u, h_send, h_recv, hr)
        sigma = 1.0 / (1.0 + jnp.exp(-hidden))
        act[t, at(u)] = (hidden * sigma).astype(BF16)
        slopes[u] = sigma * (1.0 + hidden * (1.0 - sigma))

    def give_act(u):
        tp_gather(u, act, cs, cr)

    def grade(u):
        ghid[t, at(u)] = (tp_total(u, a_send, a_recv, ar) * slopes[u]).astype(BF16)

    def give_ghid(u):
        tp_gather(u, ghid, ds, dr)

    def produce(u):
        value = dot(whole(u, act, cr), down[...])
        give_back(u, value, p_send, p_recv, ps, pr)

    def to_inputs(u):
        value = dot(whole(u, ghid, dr), up_t[...])
        give_back(u, value, q_send, q_recv, qs, qr)

    def turn(u):
        high = lax.shift_right_logical(code, 8)
        gate_hi = (high.astype(F32) * (1.0 / 128.0)).astype(BF16)
        gate_lo = ((code - high * 256).astype(F32) * (1.0 / 32768.0)).astype(BF16)
        twice = jnp.concatenate([pick.astype(F32)] * n_dp, axis=0)
        pick_t[...] = twice.T.astype(BF16)
        gates = jnp.concatenate(
            [gate_hi.astype(F32)] * n_dp + [gate_lo.astype(F32)] * n_dp, axis=0
        )
        gate_t[...] = gates.T.astype(BF16)
        up_t[...] = up[...].T
        down_t[...] = down[...].T

    def columns(buf):
        return jnp.concatenate([buf[j] for j in range(n_tp)], axis=1)

    def grad_down(u):
        gdown[0] = dot(columns(act), g_all[...], FIRST).astype(BF16)

    def grad_up(u):
        gup[0] = dot(x_all[...], columns(ghid), FIRST).astype(BF16)

    def mix(u):
        returned(p_recv, pr)
        got = join([p_recv[b] for b in range(n_blocks)])
        half = n_blocks * cap
        mixed[...] = (dot(gate_t[:, :half], got) + dot(gate_t[:, half:], got)).astype(BF16)

    def wait_up(u):
        loads[4].wait()

    def wait_down(u):
        loads[5].wait()

    def sent(u):
        for buf, sem in ((x_recv, xs), (g_recv, gs), (p_send, ps)):
            left(buf.at[pl.ds(0, len(others))], sem)
        for buf, sem in ((h_send, hs), (a_send, as_), (act, cs), (ghid, ds)):
            left(buf.at[pl.ds(0, n_tp - 1)], sem)

    steps = {
        "sent": sent,
        "up": wait_up, "down": wait_down, "h": start_hidden, "a": start_grad, "turn": turn,
        "act": activate, "ghid": grade, "p": produce, "q": to_inputs,
        "ga": give_act, "gg": give_ghid,
        "gdown": grad_down, "gup": grad_up, "mix": mix,
    }
    for name, u in plan:
        steps[name](u)
    returned(q_recv, qr)

    left(q_send.at[pl.ds(0, len(others))], qs)


STEPS = (
    "up", "h0", "down", "a0", "turn", "h1", "a1", "act0", "ghid0", "h2",
    "act1", "ga1", "a2", "act2", "ga2", "ghid1", "gg1", "p1", "ghid2", "gg2",
    "ga0", "gg0", "p2", "q1", "q2", "p0", "q0", "sent", "gdown", "gup",
    "mix",
)
SENDS = (
    "x1", "x0", "g1", "g0", "x2", "g2",
)


def spans_of(units):
    hops = [(k > 0) + (m > 0) for k, m in units]
    return [(hops.index(h), hops.count(h)) for h in sorted(set(hops))]


def pairs_of(words):
    pairs = []
    for word in words:
        name = word.rstrip("0123456789")
        pairs.append((name, int(word[len(name) :] or 0)))
    return pairs


def plan_of(units):
    spans = spans_of(units)
    sends = [
        (name, u) for name, w in pairs_of(SENDS) for u in range(spans[w][0], sum(spans[w]))[::-1]
    ]
    return spans, sends, pairs_of(STEPS)


def store(n_blocks, mixed, q_recv, pick_t, gup, gdown, mixed_o, gtok_o, gup_o, gdown_o, gtok, sem):
    copies = [
        pltpu.make_async_copy(src, dst, sem.at[i])
        for i, (src, dst) in enumerate(((gup, gup_o), (gdown, gdown_o), (mixed, mixed_o)))
    ]
    for copy in copies:
        copy.start()
    got = jnp.concatenate([q_recv[b].astype(F32) for b in range(n_blocks)], axis=0).astype(BF16)
    rows = gtok.shape[0]
    parts = 1
    step = rows // parts
    for i in range(parts):
        here = slice(i * step, (i + 1) * step)
        gtok[here] = dot(pick_t[here], got).astype(BF16)
        part = pl.ds(i * step, step)
        copy = pltpu.make_async_copy(gtok.at[part], gtok_o.at[part], sem.at[3 + i])
        copy.start()
        copies.append(copy)
    for copy in copies:
        copy.wait()


def general_kernel(
    n_dp, n_ctx, n_tp, cap,
    ids_ref, codes_ref, tok_hbm, cot_hbm, up_hbm, down_hbm,
    mixed, gtok, gup, gdown,
    tok, cot, up, down, x_send, g_send, x_recv, g_recv, x_all, g_all,
    h_send, a_send, h_recv, a_recv, act, ghid, act_all, ghid_all,
    p_send, q_send, p_recv, q_recv,
    in_sem, xs, xr, gs, gr, hs, hr, as_, ar, cs, cr, ds, dr, ps, pr, qs, qr,
):
    d, c, t = lax.axis_index("dp"), lax.axis_index("ctx"), lax.axis_index("tp")
    n_blocks = n_dp * n_ctx
    me = d * n_ctx + c
    slots = n_ctx * cap

    loads = [
        pltpu.make_async_copy(src, dst, in_sem.at[i])
        for i, (src, dst) in enumerate(
            ((tok_hbm, tok), (cot_hbm, cot), (up_hbm.at[0], up), (down_hbm.at[0], down))
        )
    ]
    for load in loads:
        load.start()

    def block_dev(k):
        b = lax.rem(me + k, n_blocks)
        return b, {"dp": b // n_ctx, "ctx": lax.rem(b, n_ctx)}

    def tp_dev(k):
        j = lax.rem(t + k, n_tp)
        return j, {"tp": j}

    barrier = pltpu.get_barrier_semaphore()
    for k in range(1, n_blocks):
        pl.semaphore_signal(barrier, inc=1, device_id=block_dev(k)[1], device_id_type=MESH)
    for k in range(1, n_tp):
        pl.semaphore_signal(barrier, inc=1, device_id=tp_dev(k)[1], device_id_type=MESH)

    picks, rows = ids_ref.shape
    lane = lax.broadcasted_iota(jnp.int32, (slots, rows), 0)
    lane_e = jnp.zeros((slots, rows), jnp.int32)
    for e in range(1, n_ctx):
        lane_e = lane_e + (lane >= e * cap).astype(jnp.int32)
    lane_s = lane - lane_e * cap
    named = jnp.zeros((slots, rows), jnp.int32)
    code = jnp.zeros((slots, rows), jnp.int32)
    ids, codes = ids_ref[...], codes_ref[...]
    for k in range(picks):
        hit = ids[k : k + 1] == lane_e
        named = jnp.where(hit, 1, named)
        code = jnp.where(hit, codes[k : k + 1], code)
    earlier = (
        lax.broadcasted_iota(jnp.int32, (rows, rows), 0)
        < lax.broadcasted_iota(jnp.int32, (rows, rows), 1)
    )
    rank = dot(named.astype(F32).astype(BF16), earlier.astype(F32).astype(BF16))
    chosen = jnp.where(rank == lane_s.astype(F32), named, 0)
    code = chosen * code
    pick = chosen.astype(F32).astype(BF16)
    high = lax.shift_right_logical(code, 8)
    gate_hi = (high.astype(F32) * (1.0 / 128.0)).astype(BF16)
    gate_lo = ((code - high * 256).astype(F32) * (1.0 / 32768.0)).astype(BF16)

    def groups_dev(g, cc):
        return {"dp": g, "ctx": cc}

    def others(k):
        return range(1 if k == 0 else 0, n_ctx)

    def to(k, m):
        return lax.rem(d + k, n_dp), lax.rem(c + m, n_ctx)

    def spread(send, recv, send_sem, recv_sem, k, back=False):
        for m in others(k):
            g, e = to(k, m)
            src = send.at[g * n_ctx + e] if back else send.at[e]
            pltpu.make_async_remote_copy(
                src, recv.at[me], send_sem.at[k * n_ctx + m], recv_sem.at[me],
                device_id=groups_dev(g, e), device_id_type=MESH,
            ).start()
        if k == 0:
            recv[me] = send[me] if back else send[c]

    def arrived(recv, recv_sem, k):
        g = lax.rem(d + n_dp - k, n_dp)
        for m in others(k):
            e = lax.rem(c + m, n_ctx)
            b = g * n_ctx + e
            pltpu.make_async_remote_copy(
                recv.at[b], recv.at[b], recv_sem.at[b], recv_sem.at[b],
                device_id=groups_dev(g, e), device_id_type=MESH,
            ).wait_recv()
        return g

    def sent(send, send_sem):
        for k in range(n_dp):
            for m in others(k):
                g, e = to(k, m)
                i = k * n_ctx + m
                pltpu.make_async_remote_copy(
                    send.at[0], send.at[0], send_sem.at[i], send_sem.at[i],
                    device_id=groups_dev(g, e), device_id_type=MESH,
                ).wait_send()

    def put_blocks(ref, first, value, count):
        for b in range(count):
            ref[first + b] = value[b * cap : (b + 1) * cap].astype(BF16)

    def take_blocks(ref, first, count):
        return jnp.concatenate(
            [ref[first + b].astype(F32) for b in range(count)], axis=0
        ).astype(BF16)

    def tp_scatter(send, recv, send_sem, recv_sem, k):
        for m in range(1, n_tp):
            j, dev = tp_dev(m)
            pltpu.make_async_remote_copy(
                send.at[k, j], recv.at[k, t], send_sem.at[k, m], recv_sem.at[k, t],
                device_id=dev, device_id_type=MESH,
            ).start()

    def tp_gather(buf, send_sem, recv_sem, k):
        for m in range(1, n_tp):
            j, dev = tp_dev(m)
            pltpu.make_async_remote_copy(
                buf.at[k, t], buf.at[k, t], send_sem.at[k, m], recv_sem.at[k, t],
                device_id=dev, device_id_type=MESH,
            ).start()

    def tp_arrived(buf, recv_sem, k):
        for m in range(1, n_tp):
            j, dev = tp_dev(m)
            pltpu.make_async_remote_copy(
                buf.at[k, j], buf.at[k, j], recv_sem.at[k, j], recv_sem.at[k, j],
                device_id=dev, device_id_type=MESH,
            ).wait_recv()

    def tp_sent(buf, send_sem):
        for k in range(n_dp):
            for m in range(1, n_tp):
                j, dev = tp_dev(m)
                pltpu.make_async_remote_copy(
                    buf.at[k, 0], buf.at[k, 0], send_sem.at[k, m], send_sem.at[k, m],
                    device_id=dev, device_id_type=MESH,
                ).wait_send()

    forth, back = list(range(n_dp)), list(reversed(range(n_dp)))
    loads[0].wait()
    put_blocks(x_send, 0, dot(pick, tok[...]), n_ctx)
    pl.semaphore_wait(barrier, n_blocks - 1 + n_tp - 1)
    for k in forth:
        spread(x_send, x_recv, xs, xr, k)
    loads[1].wait()
    put_blocks(g_send, 0, dot(gate_hi, cot[...]) + dot(gate_lo, cot[...]), n_ctx)
    for k in back:
        spread(g_send, g_recv, gs, gr, k)

    group = slots
    piece = group // n_tp

    def put_pieces(ref, k, value):
        for j in range(n_tp):
            ref[k, j] = value[j * piece : (j + 1) * piece].astype(BF16)

    def total(send, recv, k):
        value = send[k, t].astype(F32)
        for m in range(1, n_tp):
            value = value + recv[k, lax.rem(t + m, n_tp)].astype(F32)
        return value

    loads[2].wait()
    for k in forth:
        g = arrived(x_recv, xr, k)
        x_all[k * group : (k + 1) * group] = take_blocks(x_recv, g * n_ctx, n_ctx)
        put_pieces(h_send, k, dot(x_all[k * group : (k + 1) * group], up[...]))
        tp_scatter(h_send, h_recv, hs, hr, k)
    slopes = [None] * n_dp
    for k in forth:
        tp_arrived(h_recv, hr, k)
        hidden = total(h_send, h_recv, k)
        sigma = 1.0 / (1.0 + jnp.exp(-hidden))
        act[k, t] = (hidden * sigma).astype(BF16)
        tp_gather(act, cs, cr, k)
        slopes[k] = sigma * (1.0 + hidden * (1.0 - sigma))
    loads[3].wait()
    for k in back:
        g = arrived(g_recv, gr, k)
        g_all[k * group : (k + 1) * group] = take_blocks(g_recv, g * n_ctx, n_ctx)
        put_pieces(a_send, k, dot(g_all[k * group : (k + 1) * group], down[...], LAST))
        tp_scatter(a_send, a_recv, as_, ar, k)

    def whole(buf, k):
        return jnp.concatenate([buf[k, j].astype(F32) for j in range(n_tp)], axis=0).astype(BF16)

    def home(k):
        return lax.rem(d + n_dp - k, n_dp) * n_ctx, (n_dp - k) % n_dp

    for k in back:
        rows_k = slice(k * group, (k + 1) * group)
        first, to_k = home(k)
        tp_arrived(act, cr, k)
        act_all[rows_k] = whole(act, k)
        put_blocks(p_send, first, dot(act_all[rows_k], down[...]), n_ctx)
        spread(p_send, p_recv, ps, pr, to_k, back=True)
    for k in back:
        tp_arrived(a_recv, ar, k)
        ghid[k, t] = (total(a_send, a_recv, k) * slopes[k]).astype(BF16)
        tp_gather(ghid, ds, dr, k)
    for k in back:
        rows_k = slice(k * group, (k + 1) * group)
        first, to_k = home(k)
        tp_arrived(ghid, dr, k)
        ghid_all[rows_k] = whole(ghid, k)
        put_blocks(q_send, first, dot(ghid_all[rows_k], up[...], LAST), n_ctx)
        spread(q_send, q_recv, qs, qr, to_k, back=True)

    gdown[0] = dot(act_all[...], g_all[...], FIRST).astype(BF16)
    gup[0] = dot(x_all[...], ghid_all[...], FIRST).astype(BF16)

    for k in back:
        arrived(p_recv, pr, k)
    out = jnp.zeros(mixed.shape, F32)
    for g in range(n_dp):
        got = take_blocks(p_recv, g * n_ctx, n_ctx)
        out = out + dot(gate_hi, got, FIRST) + dot(gate_lo, got, FIRST)
    mixed[...] = out.astype(BF16)
    for k in back:
        arrived(q_recv, qr, k)
    out = jnp.zeros(gtok.shape, F32)
    for g in range(n_dp):
        out = out + dot(pick, take_blocks(q_recv, g * n_ctx, n_ctx), FIRST)
    gtok[...] = out.astype(BF16)

    sent(x_send, xs)
    sent(g_send, gs)
    tp_sent(h_recv, hs)
    tp_sent(a_recv, as_)
    tp_sent(act, cs)
    tp_sent(ghid, ds)
    sent(p_send, ps)
    sent(q_send, qs)


def general_store(*refs):
    sem = refs[-1]
    copies = [
        pltpu.make_async_copy(src, dst, sem.at[i])
        for i, (src, dst) in enumerate(zip(refs[:4], refs[4:8]))
    ]
    for copy in copies:
        copy.start()
    for copy in copies:
        copy.wait()


def general_body(n_dp, n_ctx, n_tp, tokens, expert_ids, gate_codes, up_weight, down_weight, cotangent):
    rows, feats = tokens.shape
    hid = up_weight.shape[2]
    cap = rows // 16
    blocks = n_dp * n_ctx
    total = blocks * cap
    piece = n_ctx * cap // n_tp
    any_ = pl.BlockSpec(memory_space=pl.ANY)
    vmem = pl.BlockSpec(memory_space=pltpu.VMEM)
    dma = pltpu.SemaphoreType.DMA

    def buf(*shape):
        return pltpu.VMEM(shape, BF16)

    tp_sems = [dma((n_dp, n_tp))] * 8
    results = pl.pallas_call(
        functools.partial(general_kernel, n_dp, n_ctx, n_tp, cap),
        out_shape=[
            buf(*a.shape) for a in (tokens, tokens, up_weight, down_weight)
        ],
        in_specs=[vmem, vmem, any_, any_, any_, any_],
        out_specs=[vmem] * 4,
        scratch_shapes=[
            buf(rows, feats), buf(rows, feats), buf(feats, hid), buf(hid, feats),
            buf(n_ctx, cap, feats), buf(n_ctx, cap, feats),
            buf(blocks, cap, feats), buf(blocks, cap, feats),
            buf(total, feats), buf(total, feats),
            buf(n_dp, n_tp, piece, hid), buf(n_dp, n_tp, piece, hid),
            buf(n_dp, n_tp, piece, hid), buf(n_dp, n_tp, piece, hid),
            buf(n_dp, n_tp, piece, hid), buf(n_dp, n_tp, piece, hid),
            buf(total, hid), buf(total, hid),
            buf(blocks, cap, feats), buf(blocks, cap, feats),
            buf(blocks, cap, feats), buf(blocks, cap, feats),
            dma((4,)),
            dma((blocks,)), dma((blocks,)), dma((blocks,)), dma((blocks,)),
            *tp_sems,
            dma((blocks,)), dma((blocks,)), dma((blocks,)), dma((blocks,)),
        ],
        compiler_params=pltpu.CompilerParams(
            collective_id=1, has_side_effects=True, vmem_limit_bytes=58 * 2**20
        ),
        name="general_expert_layer",
    )(expert_ids.T, gate_codes.T, tokens, cotangent, up_weight, down_weight)
    return tuple(
        pl.pallas_call(
            general_store,
            out_shape=[
                jax.ShapeDtypeStruct(a.shape, BF16)
                for a in (tokens, tokens, up_weight, down_weight)
            ],
            in_specs=[vmem] * 4,
            out_specs=[any_] * 4,
            scratch_shapes=[dma((4,))],
            compiler_params=pltpu.CompilerParams(vmem_limit_bytes=2**20),
            name="general_store",
        )(*[pltpu.with_memory_space_constraint(a, pltpu.VMEM) for a in results])
    )


def body(n_dp, n_ctx, n_tp, tokens, expert_ids, gate_codes, up_weight, down_weight, cotangent):
    rows, feats = tokens.shape
    hid = up_weight.shape[2]
    cap = rows // 16
    blocks = n_dp * n_ctx
    total = blocks * cap
    width = hid // n_tp
    near, units = units_of(n_dp, n_ctx)
    picks = expert_ids.shape[1]
    if width % 128 or n_tp != 4 or len(spans_of(units)) != 3 or near != CORES:
        return general_body(
            n_dp, n_ctx, n_tp, tokens, expert_ids, gate_codes, up_weight, down_weight, cotangent
        )
    any_ = pl.BlockSpec(memory_space=pl.ANY)
    vmem = pl.BlockSpec(memory_space=pltpu.VMEM)
    dma = pltpu.SemaphoreType.DMA

    def buf(*shape):
        return pltpu.VMEM(shape, BF16)

    shared, spanned = dma((1,)), dma((len(spans_of(units)),))
    results = pl.pallas_call(
        functools.partial(kernel, n_dp, n_ctx, n_tp, cap, *plan_of(units)),
        out_shape=[
            buf(rows, feats), buf(blocks, cap, feats), buf(rows, total),
            buf(*up_weight.shape), buf(*down_weight.shape),
        ],
        in_specs=[any_] * 6,
        out_specs=[vmem] * 5,
        scratch_shapes=[
            pltpu.VMEM((2, picks, rows), jnp.int32),
            buf(rows, feats), buf(rows, feats), buf(feats, hid), buf(hid, feats),
            buf(n_ctx, cap, feats), buf(n_ctx, cap, feats),
            buf(blocks, cap, feats), buf(blocks, cap, feats),
            buf(total, feats), buf(total, feats),
            *[buf(n_tp, total, width)] * 6,
            buf(blocks, cap, feats), buf(blocks, cap, feats), buf(blocks, cap, feats),
            buf(rows, 2 * total), buf(hid, feats), buf(feats, hid),
            dma((5,)),
            *[shared, spanned] * 6,
            *[shared] * 4,
        ],
        compiler_params=pltpu.CompilerParams(
            collective_id=0, has_side_effects=True, vmem_limit_bytes=58 * 2**20
        ),
        name="expert_layer",
    )(expert_ids.T, gate_codes.T, tokens, cotangent, up_weight, down_weight)
    return tuple(
        pl.pallas_call(
            functools.partial(store, blocks),
            out_shape=[
                jax.ShapeDtypeStruct(a.shape, BF16)
                for a in (tokens, tokens, up_weight, down_weight)
            ],
            in_specs=[vmem] * 5,
            out_specs=[any_] * 4,
            scratch_shapes=[buf(rows, feats), dma((4,))],
            compiler_params=pltpu.CompilerParams(vmem_limit_bytes=8 * 2**20),
            name="store",
        )(*[pltpu.with_memory_space_constraint(a, pltpu.VMEM) for a in results])
    )


def solution(mesh):
    sizes = [mesh.shape[name] for name in ("dp", "ctx", "tp")]
    return jax.shard_map(
        functools.partial(body, *sizes),
        mesh=mesh,
        in_specs=(
            P(("dp", "ctx"), "tp"),
            P(("dp", "ctx"), None),
            P(("dp", "ctx"), None),
            P("ctx", "tp", "dp"),
            P("ctx", "dp", "tp"),
            P(("dp", "ctx"), "tp"),
        ),
        out_specs=(
            P(("dp", "ctx"), "tp"),
            P(("dp", "ctx"), "tp"),
            P("ctx", "tp", "dp"),
            P("ctx", "dp", "tp"),
        ),
        check_vma=False,
    )
```
